256 devices in a mesh: scen: 16 (over x, z_lo), link: 16 (over z_hi, y, core).
Axes of the slice: x: 4, y: 4, z: 8 (z_hi: 2, z_lo: 4; z = z_hi * 4 + z_lo), core: 2. Of those that a mesh axis runs over, the one named last changes fastest.
Arguments:
- link_rows: bfloat16 [192, 2048, 4096], P('scen', None, 'link'), may hold values from -1 to 1
- slot_scenario: int32 [192, 16], P('scen'), may hold values from 0 to 162, as said below
- diag_scaling: float32 [2592, 2048], P('scen'), may hold values from 0.1 to 10
- regulariser: float32 [4096], P('link'), may hold values from 0.125 to 1
- right_side: float32 [4096], P('link'), may hold values from -6 to 6
Outputs:
- direction: float32 [4096], P('link')
- scenario_step: float32 [2592, 2048], P('scen', 'link')
The draws below stay inside these ranges and needn't reach their ends.
Inputs may be any that keep to these rules, and one draw needn't show every extreme that they name: `slot_scenario`: values of 162 mark empty slots. A scenario occupies at most one slot of a tile, and its tiles are one tile or two neighbouring tiles. In every block some tile has all 12 slots live, and at most 1 scenario of a block touches both of two neighbouring tiles; some pair of neighbouring tiles of every block reaches that number.
All inputs are finite; a program needn't handle non-finite values.
Results may differ from the reference program's by a relative error of at most 0.0029.
The reference program's roundings to bfloat16 on the way count: a program that leaves them out, or rounds other values in their place, can miss the bound.
Values may be sent and summed in bfloat16 or wider, within the bound.
A program may use at most 128 MiB of HBM per device.

```python
import math
import jax
import jax.numpy as jnp
from jax import lax

TB = 256
NV = 2048
CAP = 12
CAP2 = 1
SWEEPS = 2
TILES = 16
LROWS = 4096
SC_DEV = 162
SCEN = 2592
SLOTS = 192


mode_count = 6


def draw_link_rows(key, part):
    keys = jax.random.split(jax.random.fold_in(key, 29), 3 + mode_count)
    scale = (8.0 * NV) ** (-0.5)
    base = jnp.clip(jax.random.normal(keys[0], (SLOTS, NV, LROWS), jnp.float32), -5.0, 5.0)
    top_ratio = 30.0
    phases = jax.random.uniform(keys[1], (TILES, mode_count), jnp.float32, -math.pi, math.pi)
    ranks = jax.random.permutation(keys[2], mode_count).astype(jnp.float32)
    positions = (jnp.arange(TB, dtype=jnp.float32) + 0.5) / TB
    total = base.reshape(SLOTS, NV, TILES, TB)
    for mode in range(mode_count):
        ratio = jnp.power(jnp.float32(top_ratio), ranks[mode] / (mode_count - 1))
        strength = jnp.sqrt(ratio) * math.sqrt(2.0 / TB)
        profile = jnp.cos(math.pi * (mode + 1) * positions[None, :] + phases[:, mode][:, None])
        coeff = jnp.clip(jax.random.normal(keys[3 + mode], (SLOTS, NV, TILES), jnp.float32), -5.0, 5.0)
        total = total + strength * coeff[:, :, :, None] * profile[None, None, :, :]
    return jnp.clip(scale * total, -1.0, 1.0).reshape(SLOTS, NV, LROWS).astype(jnp.bfloat16)


def draw_slot_scenario(key, part):
    blocks_count = SCEN // SC_DEV
    keys = jax.random.split(jax.random.fold_in(key, 17), 6)
    tile_ids = jnp.arange(TILES, dtype=jnp.int32)
    loads = jax.random.randint(keys[0], (blocks_count, TILES), CAP // 2, CAP - 1)
    busy = jax.random.randint(keys[1], (blocks_count,), 0, TILES)
    loads = jnp.where(tile_ids[None, :] == busy[:, None], CAP, loads)
    shared = jax.random.randint(keys[2], (blocks_count, TILES), 0, CAP2 + 1)
    forced = jax.random.randint(keys[3], (blocks_count,), 0, TILES - 1)
    shared = jnp.where(tile_ids[None, :] == forced[:, None], CAP2, shared)
    shared = jnp.where(tile_ids[None, :] == TILES - 1, 0, shared)
    advance = loads - shared
    starts = jnp.cumsum(advance, axis=1) - advance
    slot_ids = jnp.arange(CAP, dtype=jnp.int32)
    positions = starts[:, :, None] + slot_ids[None, None, :]
    filled = slot_ids[None, None, :] < loads[:, :, None]
    orders = jax.vmap(lambda sub: jax.random.permutation(sub, SC_DEV))(jax.random.split(keys[4], blocks_count))
    safe = jnp.minimum(positions, SC_DEV - 1).reshape(blocks_count, TILES * CAP)
    named = jnp.take_along_axis(orders, safe, axis=1).reshape(blocks_count, TILES, CAP)
    named = jnp.where(filled, named, SC_DEV)
    shuffled = jax.vmap(lambda sub, row: jax.random.permutation(sub, row))(jax.random.split(keys[5], blocks_count * TILES), named.reshape(blocks_count * TILES, CAP))
    shuffled = shuffled.reshape(blocks_count, TILES, CAP)
    return jnp.transpose(shuffled, (0, 2, 1)).reshape(blocks_count * CAP, TILES).astype(jnp.int32)


def block_levels(stream_key, dims, pieces, low, largest):
    factor_of, own = 1.0, jax.random.fold_in(stream_key, 6)
    for axis_at, blocks in pieces:
        heights = jnp.exp(jax.random.uniform(jax.random.fold_in(own, axis_at), (blocks,), jnp.float32, low / len(pieces), largest / len(pieces)))
        factor_of = factor_of * jnp.repeat(heights, dims[axis_at] // blocks).reshape([-1 if axis == axis_at else 1 for axis in range(len(dims))])
    return factor_of


def bell_draw(rng, dims, spread, bound, cuts=(), kind=jnp.bfloat16):
    drawn = spread * jax.random.normal(rng, dims, jnp.float32)
    if cuts:
        drawn = drawn * block_levels(rng, dims, cuts, -0.22, 0.18)
    return jnp.clip(drawn, -bound, bound).astype(kind)


def setup_inputs(seed: int = 0) -> dict:
    arg_keys = jax.random.split(jax.random.key(seed), 6)
    return {
        "link_rows": draw_link_rows(jax.random.fold_in(arg_keys[5], 71), 0),
        "slot_scenario": draw_slot_scenario(jax.random.fold_in(arg_keys[5], 71), 0),
        "diag_scaling": jnp.clip(jnp.exp(math.log(10.0) - 4.6051702 * jax.random.uniform(arg_keys[2], (SCEN, NV), jnp.float32) ** block_levels(arg_keys[2], (SCEN, NV), ((0, 16),), -0.2, 0.2)), 0.1, 10.0),
        "regulariser": jnp.clip(jnp.exp(math.log(1.0) - 2.0794415 * jax.random.uniform(arg_keys[3], (LROWS,), jnp.float32) ** block_levels(arg_keys[3], (LROWS,), ((0, 16),), -0.2, 0.2)), 0.125, 1.0),
        "right_side": bell_draw(arg_keys[4], (LROWS,), 1.0, 6.0, ((0, 16),), jnp.float32),
    }


def straddle_select(low_ids, high_ids, allowed, scen_count, straddle_cap):
    matches = (low_ids[:, None] == high_ids[None, :]) & (low_ids[:, None] < scen_count) & allowed
    flagged = jnp.any(matches, axis=1)
    order_pos = jnp.cumsum(flagged.astype(jnp.int32)) - 1
    wanted = jnp.arange(straddle_cap, dtype=jnp.int32)
    picker = flagged[None, :] & (order_pos[None, :] == wanted[:, None])
    low_pick = picker.astype(jnp.float32)
    high_pick = jnp.dot(low_pick, matches.astype(jnp.float32), precision=lax.Precision.HIGHEST)
    return (low_pick, high_pick)

def chol_apply(factor, vector):
    column = vector[:, None]
    inner = lax.linalg.triangular_solve(factor, column, left_side=True, lower=True)
    outer = lax.linalg.triangular_solve(factor, inner, left_side=True, lower=True, transpose_a=True)
    return outer[:, 0]

def reference(link_rows, slot_scenario, diag_scaling, regulariser, right_side):
    blocks_count = SCEN // SC_DEV
    rows_tiled = link_rows.reshape(blocks_count, CAP, NV, TILES, TB)
    slot_ids = slot_scenario.reshape(blocks_count, CAP, TILES)
    scaling_blocks = diag_scaling.reshape(blocks_count, SC_DEV, NV)

    def slot_scaling(ids_here):
        live = ids_here < SC_DEV
        safe = jnp.minimum(ids_here, SC_DEV - 1)
        picked = jax.vmap(lambda table, index: jnp.take(table, index, axis=0))(scaling_blocks, safe)
        return jnp.where(live[:, :, None], picked, jnp.float32(0.0))

    def tile_terms(tile):
        tile = tile.astype(jnp.int32)
        next_tile = jnp.minimum(tile + 1, TILES - 1).astype(jnp.int32)
        allowed = tile + 1 < TILES
        ids_here = jnp.take(slot_ids, tile, axis=2)
        ids_next = jnp.take(slot_ids, next_tile, axis=2)
        here_rows = lax.dynamic_index_in_dim(rows_tiled, tile, axis=3, keepdims=False)
        next_rows = lax.dynamic_index_in_dim(rows_tiled, next_tile, axis=3, keepdims=False)
        scaled = (here_rows.astype(jnp.float32) * slot_scaling(ids_here)[:, :, :, None]).astype(jnp.bfloat16)
        scaled_wide = scaled.astype(jnp.float32)
        diag_block = jnp.einsum('bcnr,bcnq->rq', scaled_wide, here_rows.astype(jnp.float32))
        low_pick, high_pick = jax.vmap(lambda first, second: straddle_select(first, second, allowed, SC_DEV, CAP2))(ids_here, ids_next)
        own_part = jnp.einsum('bjc,bcnr->bjnr', low_pick, scaled_wide)
        far_part = jnp.einsum('bjc,bcnr->bjnr', high_pick, next_rows.astype(jnp.float32))
        upper_block = jnp.einsum('bjnr,bjnq->rq', own_part, far_part)
        return (diag_block, upper_block)
    diag_blocks, upper_blocks = lax.map(tile_terms, jnp.arange(TILES, dtype=jnp.int32))
    schur_diag = diag_blocks + jax.vmap(jnp.diag)(regulariser.reshape(TILES, TB))
    factors = jax.vmap(jnp.linalg.cholesky)(schur_diag)
    lower_blocks = jnp.concatenate([jnp.zeros((1, TB, TB), jnp.float32), jnp.swapaxes(upper_blocks[:-1], 1, 2)], axis=0)
    rhs_tiles = right_side.reshape(TILES, TB)
    parity = jnp.arange(TILES, dtype=jnp.int32) % 2
    current = jnp.zeros((TILES, TB), jnp.float32)
    edge = jnp.zeros((1, TB), jnp.float32)
    for sweep_no in range(SWEEPS):
        for colour in range(2):
            before = jnp.concatenate([edge, current[:-1]], axis=0)
            after = jnp.concatenate([current[1:], edge], axis=0)
            coupled = jnp.einsum('tab,tb->ta', lower_blocks, before, precision=lax.Precision.HIGHEST) + jnp.einsum('tab,tb->ta', upper_blocks, after, precision=lax.Precision.HIGHEST)
            solved = jax.vmap(chol_apply)(factors, rhs_tiles - coupled)
            current = jnp.where((parity == colour)[:, None], solved, current)
    half_dir = current.astype(jnp.bfloat16)
    scen_ids = jnp.arange(SC_DEV, dtype=jnp.int32)

    def add_tile(total, tile):
        tile = tile.astype(jnp.int32)
        here_rows = lax.dynamic_index_in_dim(rows_tiled, tile, axis=3, keepdims=False)
        vector = jnp.take(half_dir, tile, axis=0).astype(jnp.float32)
        values = jnp.einsum('bcnr,r->bcn', here_rows.astype(jnp.float32), vector)
        ids_here = jnp.take(slot_ids, tile, axis=2)
        picker = (scen_ids[None, :, None] == ids_here[:, None, :]).astype(jnp.float32)
        return (total + jnp.einsum('bsc,bcn->bsn', picker, values, precision=lax.Precision.HIGHEST), None)
    summed, _ = lax.scan(add_tile, jnp.zeros((blocks_count, SC_DEV, NV), jnp.float32), jnp.arange(TILES, dtype=jnp.int32))
    scenario_step = (scaling_blocks * summed).reshape(SCEN, NV)
    return (current.reshape(LROWS), scenario_step)
```

```python
import functools

import jax
import jax.numpy as jnp
from jax import lax
from jax.experimental import pallas as pl
from jax.experimental.pallas import tpu as pltpu
from jax.sharding import PartitionSpec as P

SWEEPS = 2
HALF = 128
TILE = 256
PANEL = 32
HIGHEST = lax.Precision.HIGHEST
MESH = pl.DeviceIdType.MESH
BF16 = jnp.bfloat16
F32 = jnp.float32


def dot_tt(left, right):
    return lax.dot_general(
        left, right, (((0,), (0,)), ((), ())), precision=HIGHEST, preferred_element_type=F32
    )


def tree_sum(terms):
    while len(terms) > 1:
        pairs = [terms[i] + terms[i + 1] for i in range(0, len(terms) - 1, 2)]
        terms = pairs + terms[len(terms) - len(terms) % 2 :]
    return terms[0]


def pair_sweep(held, count, first):
    second = first + 1

    def get(i, j):
        return held[(min(i, j), max(i, j))]

    a, b, c = get(first, first), get(first, second), get(second, second)
    scale = 1.0 / (a * c - b * b)
    inv_a, inv_b, inv_c = c * scale, -(b * scale), a * scale
    others = [i for i in range(count) if i not in (first, second)]
    row0 = {i: inv_a * get(first, i) + inv_b * get(second, i) for i in others}
    row1 = {i: inv_b * get(first, i) + inv_c * get(second, i) for i in others}
    new = {}
    for at, i in enumerate(others):
        for j in others[at:]:
            new[(i, j)] = get(i, j) - (get(first, i) * row0[j] + get(second, i) * row1[j])
        new[(min(i, first), max(i, first))] = row0[i]
        new[(min(i, second), max(i, second))] = row1[i]
    new[(first, first)] = -inv_a
    new[(first, second)] = -inv_b
    new[(second, second)] = -inv_c
    return new


def panel_sweep(panel, start):
    rows, width = panel.shape
    lane = lax.broadcasted_iota(jnp.int32, (1, width), 1)
    sub = lax.broadcasted_iota(jnp.int32, (8, 1), 0)

    def wide(v):
        return jnp.concatenate([v] * (width // HALF), axis=1)

    for top in range(0, rows, 8):
        at = start + top
        own = panel[top : top + 8, :]
        columns = [panel[:, at + j : at + j + 1] for j in range(8)]
        held = {}
        for j in range(8):
            spread = jnp.broadcast_to(columns[j][top : top + 8], (8, HALF))
            for i in range(j + 1):
                held[(i, j)] = jnp.broadcast_to(spread[i : i + 1], (8, HALF))
        for first in range(0, 8, 2):
            held = pair_sweep(held, 8, first)
        inverse = []
        for j in range(8):
            column = held[(0, j)]
            for i in range(1, 8):
                column = jnp.where(sub == i, held[(min(i, j), max(i, j))], column)
            inverse.append(column)
        swept = -tree_sum([wide(inverse[j]) * own[j : j + 1, :] for j in range(8)])
        for j in range(8):
            swept = jnp.where(lane == at + j, wide(inverse[j]), swept)
        inside = (lane >= at) & (lane < at + 8)
        rest = jnp.where(inside, 0.0, panel) - tree_sum(
            [columns[j] * swept[j : j + 1, :] for j in range(8)]
        )
        parts = [rest[:top]] if top else []
        parts.append(swept)
        if top + 8 < rows:
            parts.append(rest[top + 8 :])
        panel = jnp.concatenate(parts, axis=0)
    return panel


def sweep_rows(matrix, start):
    before = matrix[start : start + PANEL, :]
    after = panel_sweep(before, start)
    lane = lax.broadcasted_iota(jnp.int32, (1, TILE), 1)
    inside = (lane >= start) & (lane < start + PANEL)
    matrix[...] = jnp.where(inside, 0.0, matrix[...]) - dot_tt(before, after)
    matrix[start : start + PANEL, :] = after


def kernel(
    scens,
    links,
    ids_s,
    ids_v,
    rows_hbm,
    scaling_hbm,
    regulariser,
    right_side,
    direction_out,
    step_out,
    rows,
    scaling,
    total,
    part,
    gathered,
    full,
    matrix,
    down_rows,
    next_rows,
    upper_part,
    upper_gathered,
    upper_full,
    current,
    vec_send,
    vec_recv,
    spread,
    slot_send,
    slot_recv,
    row_sems,
    scaling_sem,
    part_send,
    part_recv,
    full_send,
    full_recv,
    next_send,
    next_recv,
    upart_send,
    upart_recv,
    ufull_send,
    ufull_recv,
    vsend_sems,
    vrecv_sems,
    slot_send_sems,
    slot_recv_sems,
):
    me_s = lax.axis_index("scen")
    me_t = lax.axis_index("link")
    slots, width, _ = rows.shape
    scen_count = scaling.shape[0]
    pieces = width // links
    chunk = part.shape[0] // scens
    uchunk = upper_part.shape[0] // scens

    def scen_peer(k):
        return lax.rem(me_s + k, scens)

    def scen_source(k):
        return lax.rem(me_s + scens - k, scens)

    def link_peer(k):
        return lax.rem(me_t + k, links)

    def link_source(k):
        return lax.rem(me_t + links - k, links)

    vec_recv[...] = jnp.zeros_like(vec_recv)
    barrier = pltpu.get_barrier_semaphore()
    for k in range(1, scens):
        pl.semaphore_signal(barrier, 1, device_id={"scen": scen_peer(k)}, device_id_type=MESH)
    for k in range(1, links):
        pl.semaphore_signal(barrier, 1, device_id={"link": link_peer(k)}, device_id_type=MESH)

    scaling_copy = pltpu.make_async_copy(scaling_hbm, scaling, scaling_sem)
    scaling_copy.start()
    for c in range(slots):
        pltpu.make_async_copy(rows_hbm.at[c], rows.at[c], row_sems.at[c]).start()

    next_t = jnp.minimum(me_t + 1, links - 1)
    prev_t = jnp.maximum(me_t - 1, 0)
    here = [ids_s[c, me_t] for c in range(slots)]
    after = [ids_s[c, next_t] for c in range(slots)]
    before = [ids_s[c, prev_t] for c in range(slots)]
    up_slot, up_found, down_slot = jnp.int32(0), jnp.int32(0), jnp.int32(0)
    for c in range(slots):
        up_hit, down_hit = jnp.int32(0), jnp.int32(0)
        for other in range(slots):
            up_hit = up_hit | (here[c] == after[other]).astype(jnp.int32)
            down_hit = down_hit | (here[c] == before[other]).astype(jnp.int32)
        live = (here[c] < scen_count).astype(jnp.int32)
        up_hit = up_hit * live
        down_hit = down_hit * live
        up_slot = jnp.where(up_hit > 0, c, up_slot)
        up_found = up_found | up_hit
        down_slot = jnp.where(down_hit > 0, c, down_slot)
    up_found = jnp.where(me_t + 1 < links, up_found, 0)

    spread[...] = jnp.zeros_like(spread)
    names = lax.broadcasted_iota(jnp.int32, (slots, TILE), 1)
    for t in range(links):
        spread[t * 16 : t * 16 + slots, :] = (ids_v[:, t : t + 1] == names).astype(F32)
    slot_send[...] = jnp.zeros_like(slot_send)

    def scale_row(name, keep):
        row = scaling[pl.ds(jnp.minimum(name, scen_count - 1), 1), :]
        return row * keep.astype(F32)

    total[...] = jnp.zeros_like(total)
    scaling_copy.wait()

    @pl.loop(0, slots)
    def _(c):
        pltpu.make_async_copy(rows_hbm.at[c], rows.at[c], row_sems.at[c]).wait()
        name = ids_s[c, me_t]
        row = scale_row(name, (name < scen_count).astype(jnp.int32))
        terms = []
        for at in range(0, width, TILE):
            block = rows[c, at : at + TILE, :]
            scaled = (block.T.astype(F32) * row[:, at : at + TILE]).astype(BF16)
            terms.append(jnp.dot(scaled, block, preferred_element_type=F32))
        summed = terms[0]
        for term in terms[1:]:
            summed = summed + term
        total[...] += summed

    low, high = total[:HALF, :HALF], total[HALF:, HALF:]
    part[:HALF, :] = 0.5 * (low + low.T)
    part[HALF : 2 * HALF, :] = 0.5 * (total[HALF:, :HALF] + total[:HALF, HALF:].T)
    part[2 * HALF :, :] = 0.5 * (high + high.T)

    pl.semaphore_wait(barrier, scens + links - 2)

    def part_copy(k):
        peer = scen_peer(k)
        return pltpu.make_async_remote_copy(
            src_ref=part.at[pl.ds(pl.multiple_of(peer * chunk, 8), chunk)],
            dst_ref=gathered.at[me_s],
            send_sem=part_send.at[k],
            recv_sem=part_recv.at[me_s],
            device_id={"scen": peer},
            device_id_type=MESH,
        )

    def part_wait(k):
        source = scen_source(k)
        pltpu.make_async_remote_copy(
            src_ref=part.at[pl.ds(0, chunk)],
            dst_ref=gathered.at[source],
            send_sem=part_send.at[k],
            recv_sem=part_recv.at[source],
            device_id={"scen": source},
            device_id_type=MESH,
        ).wait_recv()

    def full_copy(k):
        mine = pl.ds(pl.multiple_of(me_s * chunk, 8), chunk)
        return pltpu.make_async_remote_copy(
            src_ref=full.at[mine],
            dst_ref=full.at[mine],
            send_sem=full_send.at[k],
            recv_sem=full_recv.at[me_s],
            device_id={"scen": scen_peer(k)},
            device_id_type=MESH,
        )

    def full_wait(k):
        source = scen_source(k)
        theirs = pl.ds(pl.multiple_of(source * chunk, 8), chunk)
        pltpu.make_async_remote_copy(
            src_ref=full.at[theirs],
            dst_ref=full.at[theirs],
            send_sem=full_send.at[k],
            recv_sem=full_recv.at[source],
            device_id={"scen": source},
            device_id_type=MESH,
        ).wait_recv()

    def upart_copy(k):
        peer = scen_peer(k)
        return pltpu.make_async_remote_copy(
            src_ref=upper_part.at[pl.ds(pl.multiple_of(peer * uchunk, 16), uchunk)],
            dst_ref=upper_gathered.at[me_s],
            send_sem=upart_send.at[k],
            recv_sem=upart_recv.at[me_s],
            device_id={"scen": peer},
            device_id_type=MESH,
        )

    def upart_wait(k):
        source = scen_source(k)
        pltpu.make_async_remote_copy(
            src_ref=upper_part.at[pl.ds(0, uchunk)],
            dst_ref=upper_gathered.at[source],
            send_sem=upart_send.at[k],
            recv_sem=upart_recv.at[source],
            device_id={"scen": source},
            device_id_type=MESH,
        ).wait_recv()

    def ufull_copy(k):
        mine = pl.ds(pl.multiple_of(me_s * uchunk, 16), uchunk)
        return pltpu.make_async_remote_copy(
            src_ref=upper_full.at[mine],
            dst_ref=upper_full.at[mine],
            send_sem=ufull_send.at[k],
            recv_sem=ufull_recv.at[me_s],
            device_id={"scen": scen_peer(k)},
            device_id_type=MESH,
        )

    def ufull_wait(k):
        source = scen_source(k)
        theirs = pl.ds(pl.multiple_of(source * uchunk, 16), uchunk)
        pltpu.make_async_remote_copy(
            src_ref=upper_full.at[theirs],
            dst_ref=upper_full.at[theirs],
            send_sem=ufull_send.at[k],
            recv_sem=ufull_recv.at[source],
            device_id={"scen": source},
            device_id_type=MESH,
        ).wait_recv()

    @pl.loop(1, scens)
    def _(k):
        part_copy(k).start()

    @pl.loop(0, width // TILE)
    def _(j):
        at = pl.ds(pl.multiple_of(j * TILE, TILE), TILE)
        down_rows[at, :] = rows[down_slot, at, :]

    next_copy = pltpu.make_async_remote_copy(
        src_ref=down_rows,
        dst_ref=next_rows,
        send_sem=next_send,
        recv_sem=next_recv,
        device_id={"link": link_source(1)},
        device_id_type=MESH,
    )

    @pl.when(me_t > 0)
    def _():
        next_copy.start()

    gathered[me_s] = part[pl.ds(pl.multiple_of(me_s * chunk, 8), chunk), :]

    @pl.loop(1, scens)
    def _(k):
        part_wait(k)

    full[pl.ds(pl.multiple_of(me_s * chunk, 8), chunk), :] = tree_sum(
        [gathered[i] for i in range(scens)]
    )

    @pl.loop(1, scens)
    def _(k):
        full_copy(k).start()

    @pl.loop(1, scens)
    def _(k):
        full_wait(k)

    corner = full[HALF : 2 * HALF, :]
    matrix[:HALF, :HALF] = full[:HALF, :]
    matrix[HALF:, :HALF] = corner
    matrix[:HALF, HALF:] = corner.T
    matrix[HALF:, HALF:] = full[2 * HALF :, :]
    on_diag = lax.broadcasted_iota(jnp.int32, (TILE, TILE), 0) == lax.broadcasted_iota(
        jnp.int32, (TILE, TILE), 1
    )
    matrix[...] += jnp.where(on_diag, regulariser[...], 0.0)

    def upper_terms():
        @pl.when(me_t + 1 < links)
        def _():
            next_copy.wait_recv()

        @pl.when(me_t + 1 == links)
        def _():
            next_rows[...] = jnp.zeros_like(next_rows)

        row = scale_row(ids_s[up_slot, me_t], up_found)
        terms = []
        for at in range(0, width, TILE):
            block = rows[up_slot, at : at + TILE, :]
            scaled = (block.T.astype(F32) * row[:, at : at + TILE]).astype(BF16)
            terms.append(
                jnp.dot(scaled, next_rows[at : at + TILE, :], preferred_element_type=F32)
            )
        summed = tree_sum(terms).astype(BF16)
        upper_part[:TILE, :] = summed[:, :HALF]
        upper_part[TILE:, :] = summed[:, HALF:]

        @pl.loop(1, scens)
        def _(k):
            upart_copy(k).start()

        upper_gathered[me_s] = upper_part[pl.ds(pl.multiple_of(me_s * uchunk, 16), uchunk), :]

    def upper_sum():
        @pl.loop(1, scens)
        def _(k):
            upart_wait(k)

        upper_full[pl.ds(pl.multiple_of(me_s * uchunk, 16), uchunk), :] = tree_sum(
            [upper_gathered[i].astype(F32) for i in range(scens)]
        ).astype(BF16)

        @pl.loop(1, scens)
        def _(k):
            ufull_copy(k).start()

    for at in range(0, TILE, PANEL):
        sweep_rows(matrix, at)
        if at == 3 * PANEL:
            upper_terms()
        if at == 6 * PANEL:
            upper_sum()

    def solve(vector):
        wide = jnp.broadcast_to(vector, (8, TILE))
        found = -jnp.dot(wide, matrix[...], precision=HIGHEST, preferred_element_type=F32)
        return found[:1, :]

    def split(vector):
        first = vector.astype(BF16)
        left = vector - first.astype(F32)
        second = left.astype(BF16)
        third = (left - second.astype(F32)).astype(BF16)
        parts = [jnp.broadcast_to(v.astype(F32), (8, TILE)) for v in (first, second, third)]
        sub = lax.broadcasted_iota(jnp.int32, (8, TILE), 0)
        mixed = jnp.where(sub == 0, parts[0], jnp.where(sub == 1, parts[1], parts[2]))
        return jnp.where(sub < 3, mixed, 0.0).astype(BF16)

    def to_next(vector):
        parts = split(vector)
        low = jnp.dot(parts, upper_full[:TILE, :], preferred_element_type=F32)
        high = jnp.dot(parts, upper_full[TILE:, :], preferred_element_type=F32)
        return jnp.sum(jnp.concatenate([low, high], axis=1), axis=0, keepdims=True)

    def from_next(vector):
        parts = split(vector)
        turned = (((1,), (1,)), ((), ()))
        low = lax.dot_general(
            parts[:, :HALF], upper_full[:TILE, :], turned, preferred_element_type=F32
        )
        high = lax.dot_general(
            parts[:, HALF:], upper_full[TILE:, :], turned, preferred_element_type=F32
        )
        return jnp.sum(low + high, axis=0, keepdims=True)

    def put(ref, vector):
        ref[0:1, :] = vector[:, :HALF]
        ref[1:2, :] = vector[:, HALF:]

    def fetch(ref):
        return jnp.concatenate([ref[0:1, :], ref[1:2, :]], axis=1)

    def vec_copy(step, side):
        return pltpu.make_async_remote_copy(
            src_ref=vec_send.at[2 * step + side],
            dst_ref=vec_recv.at[2 * step + side],
            send_sem=vsend_sems.at[2 * step + side],
            recv_sem=vrecv_sems.at[2 * step + side],
            device_id={"link": link_source(1) if side == 0 else link_peer(1)},
            device_id_type=MESH,
        )

    colour = lax.rem(me_t, 2)
    vec_send[...] = jnp.zeros_like(vec_send)
    current[...] = jnp.zeros_like(current)

    @pl.when(colour == 0)
    def _():
        current[...] = solve(right_side[...])

    @pl.loop(1, scens)
    def _(k):
        ufull_wait(k)

    for step in range(2 * SWEEPS - 1):

        @pl.when(colour == step % 2)
        def _():
            @pl.when(me_t > 0)
            def _():
                put(vec_send.at[2 * step], current[...])
                vec_copy(step, 0).start()

            @pl.when(me_t + 1 < links)
            def _():
                put(vec_send.at[2 * step + 1], to_next(current[...]))
                vec_copy(step, 1).start()

        @pl.when(colour != step % 2)
        def _():
            @pl.when(me_t + 1 < links)
            def _():
                vec_copy(step, 0).wait_recv()

            coupled = from_next(fetch(vec_recv.at[2 * step]))

            @pl.when(me_t > 0)
            def _():
                vec_copy(step, 1).wait_recv()

            coupled = coupled + fetch(vec_recv.at[2 * step + 1])
            current[...] = solve(right_side[...] - coupled)

    direction_out[...] = current[...]

    half = jnp.broadcast_to(current[...].astype(BF16), (16, TILE))

    @pl.loop(0, slots)
    def _(c):
        for j in range(links):
            value = lax.dot_general(
                half,
                rows[c, j * pieces : (j + 1) * pieces, :],
                (((1,), (1,)), ((), ())),
                preferred_element_type=F32,
            )
            slot_send[j, pl.ds(c, 1), :] = value[:1, :]

    def slot_copy(k):
        peer = link_peer(k)
        return pltpu.make_async_remote_copy(
            src_ref=slot_send.at[peer],
            dst_ref=slot_recv.at[me_t],
            send_sem=slot_send_sems.at[k],
            recv_sem=slot_recv_sems.at[me_t],
            device_id={"link": peer},
            device_id_type=MESH,
        )

    @pl.loop(1, links)
    def _(k):
        slot_copy(k).start()

    slot_recv[me_t] = slot_send[me_t]

    @pl.loop(1, links)
    def _(k):
        source = link_source(k)
        pltpu.make_async_remote_copy(
            src_ref=slot_send.at[source],
            dst_ref=slot_recv.at[source],
            send_sem=slot_send_sems.at[k],
            recv_sem=slot_recv_sems.at[source],
            device_id={"link": source},
            device_id_type=MESH,
        ).wait_recv()

    values = slot_recv[...].reshape(links * 16, pieces)
    summed = dot_tt(spread[...], values)
    columns = scaling[:, pl.ds(pl.multiple_of(me_t * pieces, HALF), pieces)]
    step_out[...] = columns * summed[:scen_count, :]

    @pl.loop(1, scens)
    def _(k):
        part_copy(k).wait_send()
        full_copy(k).wait_send()
        upart_copy(k).wait_send()
        ufull_copy(k).wait_send()

    @pl.when(me_t > 0)
    def _():
        next_copy.wait_send()

    for step in range(2 * SWEEPS - 1):

        @pl.when(colour == step % 2)
        def _():
            @pl.when(me_t > 0)
            def _():
                vec_copy(step, 0).wait_send()

            @pl.when(me_t + 1 < links)
            def _():
                vec_copy(step, 1).wait_send()

    @pl.loop(1, links)
    def _(k):
        slot_copy(k).wait_send()


def shards(link_rows, slot_scenario, diag_scaling, regulariser, right_side):
    scens, links = lax.axis_size("scen"), lax.axis_size("link")
    slots, width, _ = link_rows.shape
    scen_count = diag_scaling.shape[0]
    pieces = width // links
    steps = 2 * SWEEPS - 1
    vmem = pl.BlockSpec(memory_space=pltpu.VMEM)
    dma = pltpu.SemaphoreType.DMA
    direction, step = pl.pallas_call(
        functools.partial(kernel, scens, links),
        out_shape=(
            jax.ShapeDtypeStruct((1, TILE), F32),
            jax.ShapeDtypeStruct((scen_count, pieces), F32),
        ),
        in_specs=[
            pl.BlockSpec(memory_space=pltpu.SMEM),
            vmem,
            pl.BlockSpec(memory_space=pl.ANY),
            pl.BlockSpec(memory_space=pl.ANY),
            vmem,
            vmem,
        ],
        out_specs=(vmem, vmem),
        scratch_shapes=[
            pltpu.VMEM((slots, width, TILE), BF16),
            pltpu.VMEM((scen_count, width), F32),
            pltpu.VMEM((TILE, TILE), F32),
            pltpu.VMEM((3 * HALF, HALF), F32),
            pltpu.VMEM((scens, 3 * HALF // scens, HALF), F32),
            pltpu.VMEM((3 * HALF, HALF), F32),
            pltpu.VMEM((TILE, TILE), F32),
            pltpu.VMEM((width, TILE), BF16),
            pltpu.VMEM((width, TILE), BF16),
            pltpu.VMEM((2 * TILE, HALF), BF16),
            pltpu.VMEM((scens, 2 * TILE // scens, HALF), BF16),
            pltpu.VMEM((2 * TILE, HALF), BF16),
            pltpu.VMEM((1, TILE), F32),
            pltpu.VMEM((2 * steps, 8, HALF), F32),
            pltpu.VMEM((2 * steps, 8, HALF), F32),
            pltpu.VMEM((links * 16, TILE), F32),
            pltpu.VMEM((links, 16, pieces), F32),
            pltpu.VMEM((links, 16, pieces), F32),
            dma((slots,)),
            dma,
            dma((scens,)),
            dma((scens,)),
            dma((scens,)),
            dma((scens,)),
            dma,
            dma,
            dma((scens,)),
            dma((scens,)),
            dma((scens,)),
            dma((scens,)),
            dma((2 * steps,)),
            dma((2 * steps,)),
            dma((links,)),
            dma((links,)),
        ],
        compiler_params=pltpu.CompilerParams(
            collective_id=0, has_side_effects=True, vmem_limit_bytes=56 * 2**20
        ),
        name="coloured_sweeps",
    )(
        slot_scenario,
        slot_scenario,
        link_rows,
        diag_scaling,
        regulariser.reshape(1, TILE),
        right_side.reshape(1, TILE),
    )
    return direction.reshape(TILE), step


def solution(mesh):
    in_specs = (P("scen", None, "link"), P("scen", None), P("scen", None), P("link"), P("link"))
    out_specs = (P("link"), P("scen", "link"))
    return jax.shard_map(shards, mesh=mesh, in_specs=in_specs, out_specs=out_specs, check_vma=False)
```

```python
import functools

import jax
import jax.numpy as jnp
from jax import lax
from jax.experimental import pallas as pl
from jax.experimental.pallas import tpu as pltpu
from jax.sharding import PartitionSpec as P

SWEEPS = 2
HALF = 128
TILE = 256
PANEL = 32
HIGHEST = lax.Precision.HIGHEST
MESH = pl.DeviceIdType.MESH
BF16 = jnp.bfloat16
F32 = jnp.float32


def dot_tt(left, right):
    return lax.dot_general(
        left, right, (((0,), (0,)), ((), ())), precision=HIGHEST, preferred_element_type=F32
    )


def tree_sum(terms):
    while len(terms) > 1:
        pairs = [terms[i] + terms[i + 1] for i in range(0, len(terms) - 1, 2)]
        terms = pairs + terms[len(terms) - len(terms) % 2 :]
    return terms[0]


def pair_sweep(held, count, first):
    second = first + 1

    def get(i, j):
        return held[(min(i, j), max(i, j))]

    a, b, c = get(first, first), get(first, second), get(second, second)
    scale = 1.0 / (a * c - b * b)
    inv_a, inv_b, inv_c = c * scale, -(b * scale), a * scale
    others = [i for i in range(count) if i not in (first, second)]
    row0 = {i: inv_a * get(first, i) + inv_b * get(second, i) for i in others}
    row1 = {i: inv_b * get(first, i) + inv_c * get(second, i) for i in others}
    new = {}
    for at, i in enumerate(others):
        for j in others[at:]:
            new[(i, j)] = get(i, j) - (get(first, i) * row0[j] + get(second, i) * row1[j])
        new[(min(i, first), max(i, first))] = row0[i]
        new[(min(i, second), max(i, second))] = row1[i]
    new[(first, first)] = -inv_a
    new[(first, second)] = -inv_b
    new[(second, second)] = -inv_c
    return new


def panel_sweep(panel, start):
    rows, width = panel.shape
    lane = lax.broadcasted_iota(jnp.int32, (1, width), 1)
    sub = lax.broadcasted_iota(jnp.int32, (8, 1), 0)

    def wide(v):
        return jnp.concatenate([v] * (width // HALF), axis=1)

    for top in range(0, rows, 8):
        at = start + top
        own = panel[top : top + 8, :]
        columns = [panel[:, at + j : at + j + 1] for j in range(8)]
        held = {}
        for j in range(8):
            spread = jnp.broadcast_to(columns[j][top : top + 8], (8, HALF))
            for i in range(j + 1):
                held[(i, j)] = jnp.broadcast_to(spread[i : i + 1], (8, HALF))
        for first in range(0, 8, 2):
            held = pair_sweep(held, 8, first)
        inverse = []
        for j in range(8):
            column = held[(0, j)]
            for i in range(1, 8):
                column = jnp.where(sub == i, held[(min(i, j), max(i, j))], column)
            inverse.append(column)
        swept = -tree_sum([wide(inverse[j]) * own[j : j + 1, :] for j in range(8)])
        for j in range(8):
            swept = jnp.where(lane == at + j, wide(inverse[j]), swept)
        inside = (lane >= at) & (lane < at + 8)
        rest = jnp.where(inside, 0.0, panel) - tree_sum(
            [columns[j] * swept[j : j + 1, :] for j in range(8)]
        )
        parts = [rest[:top]] if top else []
        parts.append(swept)
        if top + 8 < rows:
            parts.append(rest[top + 8 :])
        panel = jnp.concatenate(parts, axis=0)
    return panel


def sweep_rows(matrix, start):
    before = matrix[start : start + PANEL, :]
    after = panel_sweep(before, start)
    lane = lax.broadcasted_iota(jnp.int32, (1, TILE), 1)
    inside = (lane >= start) & (lane < start + PANEL)
    matrix[...] = jnp.where(inside, 0.0, matrix[...]) - dot_tt(before, after)
    matrix[start : start + PANEL, :] = after


def kernel(
    scens,
    links,
    ids_s,
    ids_v,
    rows_hbm,
    scaling_hbm,
    regulariser,
    right_side,
    direction_out,
    step_out,
    rows,
    scaling,
    total,
    part,
    gathered,
    full,
    matrix,
    up_keep,
    up_send,
    up_got,
    down_send,
    down_got,
    upper_part,
    below_part,
    upper_gathered,
    upper_full,
    current,
    vec_send,
    vec_recv,
    spread,
    slot_send,
    slot_recv,
    row_sems,
    scaling_sem,
    part_send,
    part_recv,
    full_send,
    full_recv,
    up_sems,
    down_sems,
    upart_send,
    upart_recv,
    bpart_send,
    bpart_recv,
    ufull_send,
    ufull_recv,
    vsend_sems,
    vrecv_sems,
    slot_send_sems,
    slot_recv_sems,
):
    me_s = lax.axis_index("scen")
    me_t = lax.axis_index("link")
    slots, width, _ = rows.shape
    scen_count = scaling.shape[0]
    pieces = width // links
    chunk = part.shape[0] // scens
    uchunk = upper_part.shape[0] // scens

    def scen_peer(k):
        return lax.rem(me_s + k, scens)

    def scen_source(k):
        return lax.rem(me_s + scens - k, scens)

    def link_peer(k):
        return lax.rem(me_t + k, links)

    def link_source(k):
        return lax.rem(me_t + links - k, links)

    scaling_copy = pltpu.make_async_copy(scaling_hbm, scaling, scaling_sem)
    scaling_copy.start()
    for c in range(slots):
        pltpu.make_async_copy(rows_hbm.at[c], rows.at[c], row_sems.at[c]).start()

    vec_recv[...] = jnp.zeros_like(vec_recv)
    barrier = pltpu.get_barrier_semaphore()

    def greet(scen, link):
        pl.semaphore_signal(
            barrier, 1, device_id={"scen": scen, "link": link}, device_id_type=MESH
        )

    @pl.loop(1, scens)
    def _(k):
        greet(scen_peer(k), me_t)
        greet(scen_peer(k), link_peer(1))
        greet(scen_peer(k), link_source(1))

    @pl.loop(1, links)
    def _(k):
        greet(me_s, link_peer(k))

    next_t = jnp.minimum(me_t + 1, links - 1)
    prev_t = jnp.maximum(me_t - 1, 0)
    here = [ids_s[c, me_t] for c in range(slots)]
    after = [ids_s[c, next_t] for c in range(slots)]
    before = [ids_s[c, prev_t] for c in range(slots)]
    up_slot, up_found, down_slot = jnp.int32(0), jnp.int32(0), jnp.int32(0)
    for c in range(slots):
        up_hit, down_hit = jnp.int32(0), jnp.int32(0)
        for other in range(slots):
            up_hit = up_hit | (here[c] == after[other]).astype(jnp.int32)
            down_hit = down_hit | (here[c] == before[other]).astype(jnp.int32)
        live = (here[c] < scen_count).astype(jnp.int32)
        up_hit = up_hit * live
        down_hit = down_hit * live
        up_slot = jnp.where(up_hit > 0, c, up_slot)
        up_found = up_found | up_hit
        down_slot = jnp.where(down_hit > 0, c, down_slot)
    up_found = jnp.where(me_t + 1 < links, up_found, 0)

    spread[...] = jnp.zeros_like(spread)
    names = lax.broadcasted_iota(jnp.int32, (slots, TILE), 1)
    for t in range(links):
        spread[t * 16 : t * 16 + slots, :] = (ids_v[:, t : t + 1] == names).astype(F32)
    slot_send[...] = jnp.zeros_like(slot_send)

    def scale_row(name, keep):
        row = scaling[pl.ds(jnp.minimum(name, scen_count - 1), 1), :]
        return row * keep.astype(F32)

    total[...] = jnp.zeros_like(total)
    scaling_copy.wait()

    def add_slot(c):
        name = ids_s[c, me_t]
        row = scale_row(name, (name < scen_count).astype(jnp.int32))
        terms = []
        for at in range(0, width, TILE):
            block = rows[c, at : at + TILE, :]
            scaled = (block.T.astype(F32) * row[:, at : at + TILE]).astype(BF16)
            terms.append(jnp.dot(scaled, block, preferred_element_type=F32))
        summed = terms[0]
        for term in terms[1:]:
            summed = summed + term
        total[...] += summed

    def arrived(c):
        pltpu.make_async_copy(rows_hbm.at[c], rows.at[c], row_sems.at[c]).wait()

    early = slots // 2

    @pl.loop(0, early)
    def _(c):
        arrived(c)
        add_slot(c)

    @pl.loop(early, slots)
    def _(c):
        arrived(c)

    part_width = width // 2
    up_row = scale_row(ids_s[up_slot, me_t], up_found)
    for at in range(0, part_width, TILE):
        down_send[at : at + TILE, :] = rows[down_slot, at : at + TILE, :]
    for at in range(0, part_width, TILE):
        beyond = part_width + at
        block = rows[up_slot, beyond : beyond + TILE, :]
        up_send[:, at : at + TILE] = (
            block.T.astype(F32) * up_row[:, beyond : beyond + TILE]
        ).astype(BF16)

    pl.semaphore_wait(barrier, 3 * (scens - 1) + links - 1)

    down_copy = pltpu.make_async_remote_copy(
        src_ref=down_send,
        dst_ref=down_got,
        send_sem=down_sems.at[0],
        recv_sem=down_sems.at[1],
        device_id={"link": link_source(1)},
        device_id_type=MESH,
    )
    up_copy = pltpu.make_async_remote_copy(
        src_ref=up_send,
        dst_ref=up_got,
        send_sem=up_sems.at[0],
        recv_sem=up_sems.at[1],
        device_id={"link": link_peer(1)},
        device_id_type=MESH,
    )

    @pl.when(me_t > 0)
    def _():
        down_copy.start()

    @pl.when(me_t + 1 < links)
    def _():
        up_copy.start()

    for at in range(0, part_width, TILE):
        block = rows[up_slot, at : at + TILE, :]
        up_keep[:, at : at + TILE] = (
            block.T.astype(F32) * up_row[:, at : at + TILE]
        ).astype(BF16)

    @pl.loop(early, slots)
    def _(c):
        add_slot(c)

    low, high = total[:HALF, :HALF], total[HALF:, HALF:]
    part[:HALF, :] = 0.5 * (low + low.T)
    part[HALF : 2 * HALF, :] = 0.5 * (total[HALF:, :HALF] + total[:HALF, HALF:].T)
    part[2 * HALF :, :] = 0.5 * (high + high.T)

    def part_copy(k):
        peer = scen_peer(k)
        return pltpu.make_async_remote_copy(
            src_ref=part.at[pl.ds(pl.multiple_of(peer * chunk, 8), chunk)],
            dst_ref=gathered.at[me_s],
            send_sem=part_send.at[k],
            recv_sem=part_recv.at[me_s],
            device_id={"scen": peer},
            device_id_type=MESH,
        )

    def part_wait(k):
        source = scen_source(k)
        pltpu.make_async_remote_copy(
            src_ref=part.at[pl.ds(0, chunk)],
            dst_ref=gathered.at[source],
            send_sem=part_send.at[k],
            recv_sem=part_recv.at[source],
            device_id={"scen": source},
            device_id_type=MESH,
        ).wait_recv()

    def full_copy(k):
        mine = pl.ds(pl.multiple_of(me_s * chunk, 8), chunk)
        return pltpu.make_async_remote_copy(
            src_ref=full.at[mine],
            dst_ref=full.at[mine],
            send_sem=full_send.at[k],
            recv_sem=full_recv.at[me_s],
            device_id={"scen": scen_peer(k)},
            device_id_type=MESH,
        )

    def full_wait(k):
        source = scen_source(k)
        theirs = pl.ds(pl.multiple_of(source * chunk, 8), chunk)
        pltpu.make_async_remote_copy(
            src_ref=full.at[theirs],
            dst_ref=full.at[theirs],
            send_sem=full_send.at[k],
            recv_sem=full_recv.at[source],
            device_id={"scen": source},
            device_id_type=MESH,
        ).wait_recv()

    def upart_copy(k):
        peer = scen_peer(k)
        return pltpu.make_async_remote_copy(
            src_ref=upper_part.at[pl.ds(pl.multiple_of(peer * uchunk, 16), uchunk)],
            dst_ref=upper_gathered.at[me_s],
            send_sem=upart_send.at[k],
            recv_sem=upart_recv.at[me_s],
            device_id={"scen": peer},
            device_id_type=MESH,
        )

    def upart_wait(k):
        source = scen_source(k)
        pltpu.make_async_remote_copy(
            src_ref=upper_part.at[pl.ds(0, uchunk)],
            dst_ref=upper_gathered.at[source],
            send_sem=upart_send.at[k],
            recv_sem=upart_recv.at[source],
            device_id={"scen": source},
            device_id_type=MESH,
        ).wait_recv()

    def bpart_copy(k):
        peer = scen_peer(k)
        return pltpu.make_async_remote_copy(
            src_ref=below_part.at[pl.ds(pl.multiple_of(peer * uchunk, 16), uchunk)],
            dst_ref=upper_gathered.at[scens + me_s],
            send_sem=bpart_send.at[k],
            recv_sem=bpart_recv.at[me_s],
            device_id={"scen": peer, "link": link_source(1)},
            device_id_type=MESH,
        )

    def bpart_wait(k):
        source = scen_source(k)
        pltpu.make_async_remote_copy(
            src_ref=below_part.at[pl.ds(0, uchunk)],
            dst_ref=upper_gathered.at[scens + source],
            send_sem=bpart_send.at[k],
            recv_sem=bpart_recv.at[source],
            device_id={"scen": source, "link": link_peer(1)},
            device_id_type=MESH,
        ).wait_recv()

    def ufull_copy(k):
        mine = pl.ds(pl.multiple_of(me_s * uchunk, 16), uchunk)
        return pltpu.make_async_remote_copy(
            src_ref=upper_full.at[mine],
            dst_ref=upper_full.at[mine],
            send_sem=ufull_send.at[k],
            recv_sem=ufull_recv.at[me_s],
            device_id={"scen": scen_peer(k)},
            device_id_type=MESH,
        )

    def ufull_wait(k):
        source = scen_source(k)
        theirs = pl.ds(pl.multiple_of(source * uchunk, 16), uchunk)
        pltpu.make_async_remote_copy(
            src_ref=upper_full.at[theirs],
            dst_ref=upper_full.at[theirs],
            send_sem=ufull_send.at[k],
            recv_sem=ufull_recv.at[source],
            device_id={"scen": source},
            device_id_type=MESH,
        ).wait_recv()

    @pl.loop(1, scens)
    def _(k):
        part_copy(k).start()

    gathered[me_s] = part[pl.ds(pl.multiple_of(me_s * chunk, 8), chunk), :]

    @pl.loop(1, scens)
    def _(k):
        part_wait(k)

    full[pl.ds(pl.multiple_of(me_s * chunk, 8), chunk), :] = tree_sum(
        [gathered[i] for i in range(scens)]
    )

    @pl.loop(1, scens)
    def _(k):
        full_copy(k).start()

    @pl.loop(1, scens)
    def _(k):
        full_wait(k)

    corner = full[HALF : 2 * HALF, :]
    matrix[:HALF, :HALF] = full[:HALF, :]
    matrix[HALF:, :HALF] = corner
    matrix[:HALF, HALF:] = corner.T
    matrix[HALF:, HALF:] = full[2 * HALF :, :]
    on_diag = lax.broadcasted_iota(jnp.int32, (TILE, TILE), 0) == lax.broadcasted_iota(
        jnp.int32, (TILE, TILE), 1
    )
    matrix[...] += jnp.where(on_diag, regulariser[...], 0.0)

    def store_wide(ref, value):
        ref[:TILE, :] = value[:, :HALF].astype(BF16)
        ref[TILE:, :] = value[:, HALF:].astype(BF16)

    def below_terms():
        @pl.when(me_t > 0)
        def _():
            up_copy.wait_recv()
            store_wide(
                below_part,
                jnp.dot(
                    up_got[...], rows[down_slot, part_width:, :], preferred_element_type=F32
                ),
            )

            @pl.loop(0, scens)
            def _(k):
                bpart_copy(k).start()

    def upper_terms():
        @pl.when(me_t + 1 < links)
        def _():
            down_copy.wait_recv()
            store_wide(
                upper_part,
                jnp.dot(up_keep[...], down_got[...], preferred_element_type=F32),
            )

            @pl.loop(1, scens)
            def _(k):
                upart_copy(k).start()

            upper_gathered[me_s] = upper_part[
                pl.ds(pl.multiple_of(me_s * uchunk, 16), uchunk), :
            ]

    def upper_sum():
        @pl.when(me_t + 1 < links)
        def _():
            @pl.loop(1, scens)
            def _(k):
                upart_wait(k)

            @pl.loop(0, scens)
            def _(k):
                bpart_wait(k)

            upper_full[pl.ds(pl.multiple_of(me_s * uchunk, 16), uchunk), :] = tree_sum(
                [upper_gathered[i].astype(F32) for i in range(2 * scens)]
            ).astype(BF16)

            @pl.loop(1, scens)
            def _(k):
                ufull_copy(k).start()

    for at in range(0, TILE, PANEL):
        sweep_rows(matrix, at)
        if at == 2 * PANEL:
            below_terms()
            upper_terms()
        if at == 6 * PANEL:
            upper_sum()

    def solve(vector):
        wide = jnp.broadcast_to(vector, (8, TILE))
        found = -jnp.dot(wide, matrix[...], precision=HIGHEST, preferred_element_type=F32)
        return found[:1, :]

    def split(vector):
        first = vector.astype(BF16)
        left = vector - first.astype(F32)
        second = left.astype(BF16)
        third = (left - second.astype(F32)).astype(BF16)
        parts = [jnp.broadcast_to(v.astype(F32), (8, TILE)) for v in (first, second, third)]
        sub = lax.broadcasted_iota(jnp.int32, (8, TILE), 0)
        mixed = jnp.where(sub == 0, parts[0], jnp.where(sub == 1, parts[1], parts[2]))
        return jnp.where(sub < 3, mixed, 0.0).astype(BF16)

    def to_next(vector):
        parts = split(vector)
        low = jnp.dot(parts, upper_full[:TILE, :], preferred_element_type=F32)
        high = jnp.dot(parts, upper_full[TILE:, :], preferred_element_type=F32)
        return jnp.sum(jnp.concatenate([low, high], axis=1), axis=0, keepdims=True)

    def from_next(vector):
        parts = split(vector)
        turned = (((1,), (1,)), ((), ()))
        low = lax.dot_general(
            parts[:, :HALF], upper_full[:TILE, :], turned, preferred_element_type=F32
        )
        high = lax.dot_general(
            parts[:, HALF:], upper_full[TILE:, :], turned, preferred_element_type=F32
        )
        return jnp.sum(low + high, axis=0, keepdims=True)

    def put(ref, vector):
        ref[0:1, :] = vector[:, :HALF]
        ref[1:2, :] = vector[:, HALF:]

    def fetch(ref):
        return jnp.concatenate([ref[0:1, :], ref[1:2, :]], axis=1)

    lane_count = 4
    seam = scens == 16 and links == 16
    lane = lax.rem(me_s, lane_count)
    first_lane = me_s - lane

    def at_seam(side):
        return me_t == links // 2 - side if seam else me_t < 0

    def vec_copy(step, side, extra):
        cross = at_seam(side)
        if extra:
            target = first_lane + jnp.where(lane == 0, 2, 1)
        else:
            target = jnp.where(cross, first_lane + lane_count - 1 - lane, me_s)
        slot = 2 * step + side
        return pltpu.make_async_remote_copy(
            src_ref=vec_send.at[slot],
            dst_ref=vec_recv.at[slot],
            send_sem=vsend_sems.at[2 * slot + extra],
            recv_sem=vrecv_sems.at[slot],
            device_id={
                "scen": target,
                "link": link_source(1) if side == 0 else link_peer(1),
            },
            device_id_type=MESH,
        )

    def vec_act(step, side, act):
        cross = at_seam(side)
        edge = (lane == 0) | (lane == lane_count - 1)

        @pl.when(jnp.logical_not(cross) | edge)
        def _():
            act(vec_copy(step, side, 0))

        if seam:

            @pl.when(cross & edge)
            def _():
                act(vec_copy(step, side, 1))

    colour = lax.rem(me_t, 2)
    vec_send[...] = jnp.zeros_like(vec_send)
    current[...] = jnp.zeros_like(current)

    @pl.when(colour == 0)
    def _():
        current[...] = solve(right_side[...])

    @pl.when(me_t + 1 < links)
    def _():
        @pl.loop(1, scens)
        def _(k):
            ufull_wait(k)

    for step in range(2 * SWEEPS - 1):

        @pl.when(colour == step % 2)
        def _():
            @pl.when(me_t > 0)
            def _():
                put(vec_send.at[2 * step], current[...])
                vec_act(step, 0, lambda copy: copy.start())

            @pl.when(me_t + 1 < links)
            def _():
                put(vec_send.at[2 * step + 1], to_next(current[...]))
                vec_act(step, 1, lambda copy: copy.start())

        @pl.when(colour != step % 2)
        def _():
            current[...] = right_side[...]

            @pl.when(me_t + 1 < links)
            def _():
                vec_copy(step, 0, 0).wait_recv()
                current[...] -= from_next(fetch(vec_recv.at[2 * step]))

            @pl.when(me_t > 0)
            def _():
                vec_copy(step, 1, 0).wait_recv()
                current[...] -= fetch(vec_recv.at[2 * step + 1])

            current[...] = solve(current[...])

    direction_out[...] = current[...]

    half = jnp.broadcast_to(current[...].astype(BF16), (16, TILE))

    @pl.loop(0, slots)
    def _(c):
        for j in range(links):
            value = lax.dot_general(
                half,
                rows[c, j * pieces : (j + 1) * pieces, :],
                (((1,), (1,)), ((), ())),
                preferred_element_type=F32,
            )
            slot_send[j, pl.ds(c, 1), :] = value[:1, :]

    def slot_copy(k):
        peer = link_peer(k)
        return pltpu.make_async_remote_copy(
            src_ref=slot_send.at[peer],
            dst_ref=slot_recv.at[me_t],
            send_sem=slot_send_sems.at[k],
            recv_sem=slot_recv_sems.at[me_t],
            device_id={"link": peer},
            device_id_type=MESH,
        )

    @pl.loop(1, links)
    def _(k):
        slot_copy(k).start()

    slot_recv[me_t] = slot_send[me_t]

    @pl.loop(1, links)
    def _(k):
        source = link_source(k)
        pltpu.make_async_remote_copy(
            src_ref=slot_send.at[source],
            dst_ref=slot_recv.at[source],
            send_sem=slot_send_sems.at[k],
            recv_sem=slot_recv_sems.at[source],
            device_id={"link": source},
            device_id_type=MESH,
        ).wait_recv()

    values = slot_recv[...].reshape(links * 16, pieces)
    summed = dot_tt(spread[...], values)
    columns = scaling[:, pl.ds(pl.multiple_of(me_t * pieces, HALF), pieces)]
    step_out[...] = columns * summed[:scen_count, :]

    @pl.loop(1, scens)
    def _(k):
        part_copy(k).wait_send()
        full_copy(k).wait_send()

    @pl.when(me_t + 1 < links)
    def _():
        up_copy.wait_send()

        @pl.loop(1, scens)
        def _(k):
            upart_copy(k).wait_send()
            ufull_copy(k).wait_send()

    @pl.when(me_t > 0)
    def _():
        down_copy.wait_send()

        @pl.loop(0, scens)
        def _(k):
            bpart_copy(k).wait_send()

    for step in range(2 * SWEEPS - 1):

        @pl.when(colour == step % 2)
        def _():
            @pl.when(me_t > 0)
            def _():
                vec_act(step, 0, lambda copy: copy.wait_send())

            @pl.when(me_t + 1 < links)
            def _():
                vec_act(step, 1, lambda copy: copy.wait_send())

    @pl.loop(1, links)
    def _(k):
        slot_copy(k).wait_send()


def shards(link_rows, slot_scenario, diag_scaling, regulariser, right_side):
    scens, links = lax.axis_size("scen"), lax.axis_size("link")
    slots, width, _ = link_rows.shape
    scen_count = diag_scaling.shape[0]
    pieces = width // links
    steps = 2 * SWEEPS - 1
    vmem = pl.BlockSpec(memory_space=pltpu.VMEM)
    dma = pltpu.SemaphoreType.DMA
    direction, step = pl.pallas_call(
        functools.partial(kernel, scens, links),
        out_shape=(
            jax.ShapeDtypeStruct((1, TILE), F32),
            jax.ShapeDtypeStruct((scen_count, pieces), F32),
        ),
        in_specs=[
            pl.BlockSpec(memory_space=pltpu.SMEM),
            vmem,
            pl.BlockSpec(memory_space=pl.ANY),
            pl.BlockSpec(memory_space=pl.ANY),
            vmem,
            vmem,
        ],
        out_specs=(vmem, vmem),
        scratch_shapes=[
            pltpu.VMEM((slots, width, TILE), BF16),
            pltpu.VMEM((scen_count, width), F32),
            pltpu.VMEM((TILE, TILE), F32),
            pltpu.VMEM((3 * HALF, HALF), F32),
            pltpu.VMEM((scens, 3 * HALF // scens, HALF), F32),
            pltpu.VMEM((3 * HALF, HALF), F32),
            pltpu.VMEM((TILE, TILE), F32),
            pltpu.VMEM((TILE, width // 2), BF16),
            pltpu.VMEM((TILE, width // 2), BF16),
            pltpu.VMEM((TILE, width // 2), BF16),
            pltpu.VMEM((width // 2, TILE), BF16),
            pltpu.VMEM((width // 2, TILE), BF16),
            pltpu.VMEM((2 * TILE, HALF), BF16),
            pltpu.VMEM((2 * TILE, HALF), BF16),
            pltpu.VMEM((2 * scens, 2 * TILE // scens, HALF), BF16),
            pltpu.VMEM((2 * TILE, HALF), BF16),
            pltpu.VMEM((1, TILE), F32),
            pltpu.VMEM((2 * steps, 8, HALF), F32),
            pltpu.VMEM((2 * steps, 8, HALF), F32),
            pltpu.VMEM((links * 16, TILE), F32),
            pltpu.VMEM((links, 16, pieces), F32),
            pltpu.VMEM((links, 16, pieces), F32),
            dma((slots,)),
            dma,
            dma((scens,)),
            dma((scens,)),
            dma((scens,)),
            dma((scens,)),
            dma((2,)),
            dma((2,)),
            dma((scens,)),
            dma((scens,)),
            dma((scens,)),
            dma((scens,)),
            dma((scens,)),
            dma((scens,)),
            dma((4 * steps,)),
            dma((2 * steps,)),
            dma((links,)),
            dma((links,)),
        ],
        compiler_params=pltpu.CompilerParams(
            collective_id=0, has_side_effects=True, vmem_limit_bytes=56 * 2**20
        ),
        name="coloured_sweeps",
    )(
        slot_scenario,
        slot_scenario,
        link_rows,
        diag_scaling,
        regulariser.reshape(1, TILE),
        right_side.reshape(1, TILE),
    )
    return direction.reshape(TILE), step


def solution(mesh):
    in_specs = (P("scen", None, "link"), P("scen", None), P("scen", None), P("link"), P("link"))
    out_specs = (P("link"), P("scen", "link"))
    return jax.shard_map(shards, mesh=mesh, in_specs=in_specs, out_specs=out_specs, check_vma=False)
```

```python
import functools

import jax
import jax.numpy as jnp
from jax import lax
from jax.experimental import pallas as pl
from jax.experimental.pallas import tpu as pltpu
from jax.sharding import PartitionSpec as P

SWEEPS = 2
HALF = 128
AHEAD = 3
PIECES = 8
SEAM_TURN = 4
FIRST, SECOND = 2, 4
TILE = 256
PANEL = 32
HIGHEST = lax.Precision.HIGHEST
MESH = pl.DeviceIdType.MESH
BF16 = jnp.bfloat16
F32 = jnp.float32


def dot_tt(left, right):
    return lax.dot_general(
        left, right, (((0,), (0,)), ((), ())), precision=HIGHEST, preferred_element_type=F32
    )


def tree_sum(terms):
    while len(terms) > 1:
        pairs = [terms[i] + terms[i + 1] for i in range(0, len(terms) - 1, 2)]
        terms = pairs + terms[len(terms) - len(terms) % 2 :]
    return terms[0]


def pair_sweep(held, count, first):
    second = first + 1

    def get(i, j):
        return held[(min(i, j), max(i, j))]

    a, b, c = get(first, first), get(first, second), get(second, second)
    scale = 1.0 / (a * c - b * b)
    inv_a, inv_b, inv_c = c * scale, -(b * scale), a * scale
    others = [i for i in range(count) if i not in (first, second)]
    row0 = {i: inv_a * get(first, i) + inv_b * get(second, i) for i in others}
    row1 = {i: inv_b * get(first, i) + inv_c * get(second, i) for i in others}
    new = {}
    for at, i in enumerate(others):
        for j in others[at:]:
            new[(i, j)] = get(i, j) - (get(first, i) * row0[j] + get(second, i) * row1[j])
        new[(min(i, first), max(i, first))] = row0[i]
        new[(min(i, second), max(i, second))] = row1[i]
    new[(first, first)] = -inv_a
    new[(first, second)] = -inv_b
    new[(second, second)] = -inv_c
    return new


def panel_sweep(panel, start):
    rows, width = panel.shape
    lane = lax.broadcasted_iota(jnp.int32, (1, width), 1)
    sub = lax.broadcasted_iota(jnp.int32, (8, 1), 0)

    def wide(v):
        return jnp.concatenate([v] * (width // HALF), axis=1)

    for top in range(0, rows, 8):
        at = start + top
        own = panel[top : top + 8, :]
        columns = [panel[:, at + j : at + j + 1] for j in range(8)]
        held = {}
        for j in range(8):
            spread = jnp.broadcast_to(columns[j][top : top + 8], (8, HALF))
            for i in range(j + 1):
                held[(i, j)] = jnp.broadcast_to(spread[i : i + 1], (8, HALF))
        for first in range(0, 8, 2):
            held = pair_sweep(held, 8, first)
        inverse = []
        for j in range(8):
            column = held[(0, j)]
            for i in range(1, 8):
                column = jnp.where(sub == i, held[(min(i, j), max(i, j))], column)
            inverse.append(column)
        swept = -tree_sum([wide(inverse[j]) * own[j : j + 1, :] for j in range(8)])
        for j in range(8):
            swept = jnp.where(lane == at + j, wide(inverse[j]), swept)
        inside = (lane >= at) & (lane < at + 8)
        rest = jnp.where(inside, 0.0, panel) - tree_sum(
            [columns[j] * swept[j : j + 1, :] for j in range(8)]
        )
        parts = [rest[:top]] if top else []
        parts.append(swept)
        if top + 8 < rows:
            parts.append(rest[top + 8 :])
        panel = jnp.concatenate(parts, axis=0)
    return panel


def sweep_rows(matrix, start):
    before = matrix[start : start + PANEL, :]
    after = panel_sweep(before, start)
    lane = lax.broadcasted_iota(jnp.int32, (1, TILE), 1)
    inside = (lane >= start) & (lane < start + PANEL)
    matrix[...] = jnp.where(inside, 0.0, matrix[...]) - dot_tt(before, after)
    matrix[start : start + PANEL, :] = after


def kernel(
    scens,
    links,
    ids_s,
    ids_v,
    rows_hbm,
    scaling_hbm,
    regulariser,
    right_side,
    direction_out,
    step_out,
    rows,
    scaling,
    total,
    part,
    gathered,
    full,
    matrix,
    up_keep,
    up_send,
    up_got,
    down_send,
    down_got,
    upper_part,
    below_part,
    upper_gathered,
    upper_full,
    current,
    vec_send,
    vec_recv,
    spread,
    slot_send,
    slot_recv,
    row_sems,
    scaling_sem,
    part_send,
    part_recv,
    full_send,
    full_recv,
    up_sems,
    down_sems,
    upart_send,
    upart_recv,
    bpart_send,
    bpart_recv,
    ufull_send,
    ufull_recv,
    vsend_sems,
    vrecv_sems,
    slot_send_sems,
    slot_recv_sems,
):
    me_s = lax.axis_index("scen")
    me_t = lax.axis_index("link")
    slots, width, _ = rows.shape
    scen_count = scaling.shape[0]
    pieces = width // links
    chunk = part.shape[0] // scens
    uchunk = upper_part.shape[0] // scens

    def scen_peer(k):
        return lax.rem(me_s + k, scens)

    def scen_source(k):
        return lax.rem(me_s + scens - k, scens)

    def link_peer(k):
        return lax.rem(me_t + k, links)

    def link_source(k):
        return lax.rem(me_t + links - k, links)

    scaling_copy = pltpu.make_async_copy(scaling_hbm, scaling, scaling_sem)
    scaling_copy.start()

    def row_copy(c):
        return pltpu.make_async_copy(rows_hbm.at[c], rows.at[c], row_sems.at[c])

    for c in range(AHEAD):
        row_copy(c).start()

    vec_recv[...] = jnp.zeros_like(vec_recv)
    barrier = pltpu.get_barrier_semaphore()

    def greet(scen, link):
        pl.semaphore_signal(
            barrier, 1, device_id={"scen": scen, "link": link}, device_id_type=MESH
        )

    @pl.loop(1, scens)
    def _(k):
        greet(scen_peer(k), me_t)
        greet(scen_peer(k), link_peer(1))
        greet(scen_peer(k), link_source(1))

    @pl.loop(1, links)
    def _(k):
        greet(me_s, link_peer(k))

    next_t = jnp.minimum(me_t + 1, links - 1)
    prev_t = jnp.maximum(me_t - 1, 0)
    here = [ids_s[c, me_t] for c in range(slots)]
    after = [ids_s[c, next_t] for c in range(slots)]
    before = [ids_s[c, prev_t] for c in range(slots)]
    up_slot, up_found, down_slot = jnp.int32(0), jnp.int32(0), jnp.int32(0)
    for c in range(slots):
        up_hit, down_hit = jnp.int32(0), jnp.int32(0)
        for other in range(slots):
            up_hit = up_hit | (here[c] == after[other]).astype(jnp.int32)
            down_hit = down_hit | (here[c] == before[other]).astype(jnp.int32)
        live = (here[c] < scen_count).astype(jnp.int32)
        up_hit = up_hit * live
        down_hit = down_hit * live
        up_slot = jnp.where(up_hit > 0, c, up_slot)
        up_found = up_found | up_hit
        down_slot = jnp.where(down_hit > 0, c, down_slot)
    up_found = jnp.where(me_t + 1 < links, up_found, 0)

    spread[...] = jnp.zeros_like(spread)
    names = lax.broadcasted_iota(jnp.int32, (slots, TILE), 1)
    for t in range(links):
        spread[t * 16 : t * 16 + slots, :] = (ids_v[:, t : t + 1] == names).astype(F32)

    def scale_row(name, keep):
        row = scaling[pl.ds(jnp.minimum(name, scen_count - 1), 1), :]
        return row * keep.astype(F32)

    total[...] = jnp.zeros_like(total)
    scaling_copy.wait()

    def add_slot(c):
        name = ids_s[c, me_t]
        row = scale_row(name, (name < scen_count).astype(jnp.int32))
        terms = []
        for at in range(0, width, TILE):
            block = rows[c, at : at + TILE, :]
            scaled = (block.T.astype(F32) * row[:, at : at + TILE]).astype(BF16)
            terms.append(jnp.dot(scaled, block, preferred_element_type=F32))
        summed = terms[0]
        for term in terms[1:]:
            summed = summed + term
        total[...] += summed

    def arrived(c):
        row_copy(c).wait()

        @pl.when(c + AHEAD < slots)
        def _():
            row_copy(c + AHEAD).start()

    early = slots - AHEAD

    @pl.loop(0, early)
    def _(c):
        arrived(c)
        add_slot(c)

    @pl.loop(early, slots)
    def _(c):
        arrived(c)

    part_width = width // 2
    up_row = scale_row(ids_s[up_slot, me_t], up_found)
    for at in range(0, part_width, TILE):
        down_send[at : at + TILE, :] = rows[down_slot, at : at + TILE, :]
    for at in range(0, part_width, TILE):
        beyond = part_width + at
        block = rows[up_slot, beyond : beyond + TILE, :]
        scaled = (block.T.astype(F32) * up_row[:, beyond : beyond + TILE]).astype(BF16)
        for inner in range(0, TILE, part_width // PIECES):
            up_send[(at + inner) // (part_width // PIECES)] = scaled[
                :, inner : inner + part_width // PIECES
            ]

    pl.semaphore_wait(barrier, 3 * (scens - 1) + links - 1)

    piece = part_width // PIECES
    seam = scens == 16 and links == 16

    def at_seam(side):
        return (me_t == links // 2 - side) if seam else (me_t < 0)

    def row_pieces(side, at, count):
        if side == 0:
            span = pl.ds(at * piece, count * piece)
            source, target = down_send.at[span], down_got.at[span]
            sems, peer = down_sems, link_source(1)
        else:
            span = pl.ds(at, count)
            source, target = up_send.at[span], up_got.at[span]
            sems, peer = up_sems, link_peer(1)
        return pltpu.make_async_remote_copy(
            src_ref=source,
            dst_ref=target,
            send_sem=sems.at[0],
            recv_sem=sems.at[1],
            device_id={"link": peer},
            device_id_type=MESH,
        )

    down_copy = row_pieces(0, 0, PIECES)
    up_copy = row_pieces(1, 0, PIECES)

    def seam_rows(first, last):
        for side in range(2):

            @pl.when(at_seam(side))
            def _():
                for at in range(first, last):
                    row_pieces(side, at, 1).start()

    @pl.when((me_t > 0) & jnp.logical_not(at_seam(0)))
    def _():
        down_copy.start()

    @pl.when((me_t + 1 < links) & jnp.logical_not(at_seam(1)))
    def _():
        up_copy.start()

    if seam:
        seam_rows(0, FIRST)

    for at in range(0, part_width, TILE):
        block = rows[up_slot, at : at + TILE, :]
        up_keep[:, at : at + TILE] = (
            block.T.astype(F32) * up_row[:, at : at + TILE]
        ).astype(BF16)

    @pl.loop(early, slots)
    def _(c):
        add_slot(c)

    low, high = total[:HALF, :HALF], total[HALF:, HALF:]
    part[:HALF, :] = 0.5 * (low + low.T)
    part[HALF : 2 * HALF, :] = 0.5 * (total[HALF:, :HALF] + total[:HALF, HALF:].T)
    part[2 * HALF :, :] = 0.5 * (high + high.T)

    def part_copy(k):
        peer = scen_peer(k)
        return pltpu.make_async_remote_copy(
            src_ref=part.at[pl.ds(pl.multiple_of(peer * chunk, 8), chunk)],
            dst_ref=gathered.at[me_s],
            send_sem=part_send.at[k],
            recv_sem=part_recv.at[me_s],
            device_id={"scen": peer},
            device_id_type=MESH,
        )

    def part_wait(k):
        source = scen_source(k)
        pltpu.make_async_remote_copy(
            src_ref=part.at[pl.ds(0, chunk)],
            dst_ref=gathered.at[source],
            send_sem=part_send.at[k],
            recv_sem=part_recv.at[source],
            device_id={"scen": source},
            device_id_type=MESH,
        ).wait_recv()

    def full_copy(k):
        mine = pl.ds(pl.multiple_of(me_s * chunk, 8), chunk)
        return pltpu.make_async_remote_copy(
            src_ref=full.at[mine],
            dst_ref=full.at[mine],
            send_sem=full_send.at[k],
            recv_sem=full_recv.at[me_s],
            device_id={"scen": scen_peer(k)},
            device_id_type=MESH,
        )

    def full_wait(k):
        source = scen_source(k)
        theirs = pl.ds(pl.multiple_of(source * chunk, 8), chunk)
        pltpu.make_async_remote_copy(
            src_ref=full.at[theirs],
            dst_ref=full.at[theirs],
            send_sem=full_send.at[k],
            recv_sem=full_recv.at[source],
            device_id={"scen": source},
            device_id_type=MESH,
        ).wait_recv()

    def upart_copy(k):
        peer = scen_peer(k)
        return pltpu.make_async_remote_copy(
            src_ref=upper_part.at[pl.ds(pl.multiple_of(peer * uchunk, 16), uchunk)],
            dst_ref=upper_gathered.at[me_s],
            send_sem=upart_send.at[k],
            recv_sem=upart_recv.at[me_s],
            device_id={"scen": peer},
            device_id_type=MESH,
        )

    def upart_wait(k):
        source = scen_source(k)
        pltpu.make_async_remote_copy(
            src_ref=upper_part.at[pl.ds(0, uchunk)],
            dst_ref=upper_gathered.at[source],
            send_sem=upart_send.at[k],
            recv_sem=upart_recv.at[source],
            device_id={"scen": source},
            device_id_type=MESH,
        ).wait_recv()

    def bpart_copy(k):
        peer = scen_peer(k)
        return pltpu.make_async_remote_copy(
            src_ref=below_part.at[pl.ds(pl.multiple_of(peer * uchunk, 16), uchunk)],
            dst_ref=upper_gathered.at[scens + me_s],
            send_sem=bpart_send.at[k],
            recv_sem=bpart_recv.at[me_s],
            device_id={"scen": peer, "link": link_source(1)},
            device_id_type=MESH,
        )

    def bpart_wait(k):
        source = scen_source(k)
        pltpu.make_async_remote_copy(
            src_ref=below_part.at[pl.ds(0, uchunk)],
            dst_ref=upper_gathered.at[scens + source],
            send_sem=bpart_send.at[k],
            recv_sem=bpart_recv.at[source],
            device_id={"scen": source, "link": link_peer(1)},
            device_id_type=MESH,
        ).wait_recv()

    def ufull_copy(k):
        mine = pl.ds(pl.multiple_of(me_s * uchunk, 16), uchunk)
        return pltpu.make_async_remote_copy(
            src_ref=upper_full.at[mine],
            dst_ref=upper_full.at[mine],
            send_sem=ufull_send.at[k],
            recv_sem=ufull_recv.at[me_s],
            device_id={"scen": scen_peer(k)},
            device_id_type=MESH,
        )

    def ufull_wait(k):
        source = scen_source(k)
        theirs = pl.ds(pl.multiple_of(source * uchunk, 16), uchunk)
        pltpu.make_async_remote_copy(
            src_ref=upper_full.at[theirs],
            dst_ref=upper_full.at[theirs],
            send_sem=ufull_send.at[k],
            recv_sem=ufull_recv.at[source],
            device_id={"scen": source},
            device_id_type=MESH,
        ).wait_recv()

    @pl.loop(1, scens)
    def _(k):
        part_copy(k).start()

    if seam:
        seam_rows(FIRST, SECOND)

    gathered[me_s] = part[pl.ds(pl.multiple_of(me_s * chunk, 8), chunk), :]

    @pl.loop(1, scens)
    def _(k):
        part_wait(k)

    full[pl.ds(pl.multiple_of(me_s * chunk, 8), chunk), :] = tree_sum(
        [gathered[i] for i in range(scens)]
    )

    @pl.loop(1, scens)
    def _(k):
        full_copy(k).start()

    if seam:
        seam_rows(SECOND, PIECES)

    @pl.loop(1, scens)
    def _(k):
        full_wait(k)

    corner = full[HALF : 2 * HALF, :]
    matrix[:HALF, :HALF] = full[:HALF, :]
    matrix[HALF:, :HALF] = corner
    matrix[:HALF, HALF:] = corner.T
    matrix[HALF:, HALF:] = full[2 * HALF :, :]
    on_diag = lax.broadcasted_iota(jnp.int32, (TILE, TILE), 0) == lax.broadcasted_iota(
        jnp.int32, (TILE, TILE), 1
    )
    matrix[...] += jnp.where(on_diag, regulariser[...], 0.0)

    def store_wide(ref, value):
        ref[:TILE, :] = value[:, :HALF].astype(BF16)
        ref[TILE:, :] = value[:, HALF:].astype(BF16)

    def below_terms():
        @pl.when(me_t > 0)
        def _():
            up_copy.wait_recv()
            scaled = jnp.concatenate([up_got[i] for i in range(PIECES)], axis=1)
            store_wide(
                below_part,
                jnp.dot(scaled, rows[down_slot, part_width:, :], preferred_element_type=F32),
            )

            @pl.loop(0, scens)
            def _(k):
                bpart_copy(k).start()

    def upper_terms():
        @pl.when(me_t + 1 < links)
        def _():
            down_copy.wait_recv()
            store_wide(
                upper_part,
                jnp.dot(up_keep[...], down_got[...], preferred_element_type=F32),
            )

            @pl.loop(1, scens)
            def _(k):
                upart_copy(k).start()

            upper_gathered[me_s] = upper_part[
                pl.ds(pl.multiple_of(me_s * uchunk, 16), uchunk), :
            ]

    def upper_sum():
        @pl.when(me_t + 1 < links)
        def _():
            @pl.loop(1, scens)
            def _(k):
                upart_wait(k)

            @pl.loop(0, scens)
            def _(k):
                bpart_wait(k)

            upper_full[pl.ds(pl.multiple_of(me_s * uchunk, 16), uchunk), :] = tree_sum(
                [upper_gathered[i].astype(F32) for i in range(2 * scens)]
            ).astype(BF16)

            @pl.loop(1, scens)
            def _(k):
                ufull_copy(k).start()

    for at in range(0, TILE, PANEL):
        sweep_rows(matrix, at)
        for turn, late in ((0, False), (SEAM_TURN, True)):
            if at == turn * PANEL and (seam or not late):
                pl.when(at_seam(0) == late)(below_terms)
                pl.when(at_seam(1) == late)(upper_terms)
        if at == 4 * PANEL:
            pl.when(jnp.logical_not(at_seam(1)))(upper_sum)

    if seam:
        pl.when(at_seam(1))(upper_sum)

    def solve(vector):
        wide = jnp.broadcast_to(vector, (8, TILE))
        found = -jnp.dot(wide, matrix[...], precision=HIGHEST, preferred_element_type=F32)
        return found[:1, :]

    def split(vector):
        first = vector.astype(BF16)
        left = vector - first.astype(F32)
        second = left.astype(BF16)
        third = (left - second.astype(F32)).astype(BF16)
        parts = [jnp.broadcast_to(v.astype(F32), (8, TILE)) for v in (first, second, third)]
        sub = lax.broadcasted_iota(jnp.int32, (8, TILE), 0)
        mixed = jnp.where(sub == 0, parts[0], jnp.where(sub == 1, parts[1], parts[2]))
        return jnp.where(sub < 3, mixed, 0.0).astype(BF16)

    def to_next(vector):
        parts = split(vector)
        low = jnp.dot(parts, upper_full[:TILE, :], preferred_element_type=F32)
        high = jnp.dot(parts, upper_full[TILE:, :], preferred_element_type=F32)
        return jnp.sum(jnp.concatenate([low, high], axis=1), axis=0, keepdims=True)

    def from_next(vector):
        parts = split(vector)
        turned = (((1,), (1,)), ((), ()))
        low = lax.dot_general(
            parts[:, :HALF], upper_full[:TILE, :], turned, preferred_element_type=F32
        )
        high = lax.dot_general(
            parts[:, HALF:], upper_full[TILE:, :], turned, preferred_element_type=F32
        )
        return jnp.sum(low + high, axis=0, keepdims=True)

    def put(ref, vector):
        ref[0:1, :] = vector[:, :HALF]
        ref[1:2, :] = vector[:, HALF:]

    def fetch(ref):
        return jnp.concatenate([ref[0:1, :], ref[1:2, :]], axis=1)

    lane_count = 4
    lane = lax.rem(me_s, lane_count)
    first_lane = me_s - lane

    def vec_copy(step, side, extra):
        cross = at_seam(side)
        if extra:
            target = first_lane + jnp.where(lane == 0, 2, 1)
        else:
            target = jnp.where(cross, first_lane + lane_count - 1 - lane, me_s)
        slot = 2 * step + side
        return pltpu.make_async_remote_copy(
            src_ref=vec_send.at[slot],
            dst_ref=vec_recv.at[slot],
            send_sem=vsend_sems.at[2 * slot + extra],
            recv_sem=vrecv_sems.at[slot],
            device_id={
                "scen": target,
                "link": link_source(1) if side == 0 else link_peer(1),
            },
            device_id_type=MESH,
        )

    def vec_act(step, side, act):
        cross = at_seam(side)
        edge = (lane == 0) | (lane == lane_count - 1)

        @pl.when(jnp.logical_not(cross) | edge)
        def _():
            act(vec_copy(step, side, 0))

        if seam:

            @pl.when(cross & edge)
            def _():
                act(vec_copy(step, side, 1))

    colour = lax.rem(me_t, 2)
    vec_send[...] = jnp.zeros_like(vec_send)
    current[...] = jnp.zeros_like(current)

    @pl.when(colour == 0)
    def _():
        current[...] = solve(right_side[...])

    @pl.when(me_t + 1 < links)
    def _():
        @pl.loop(1, scens)
        def _(k):
            ufull_wait(k)

    for step in range(2 * SWEEPS - 1):

        @pl.when(colour == step % 2)
        def _():
            @pl.when(me_t > 0)
            def _():
                put(vec_send.at[2 * step], current[...])
                vec_act(step, 0, lambda copy: copy.start())

            @pl.when(me_t + 1 < links)
            def _():
                put(vec_send.at[2 * step + 1], to_next(current[...]))
                vec_act(step, 1, lambda copy: copy.start())

        @pl.when(colour != step % 2)
        def _():
            current[...] = right_side[...]

            @pl.when(me_t + 1 < links)
            def _():
                vec_copy(step, 0, 0).wait_recv()
                current[...] -= from_next(fetch(vec_recv.at[2 * step]))

            @pl.when(me_t > 0)
            def _():
                vec_copy(step, 1, 0).wait_recv()
                current[...] -= fetch(vec_recv.at[2 * step + 1])

            current[...] = solve(current[...])

    direction_out[...] = current[...]

    rounded = current[...].astype(BF16)
    half = jnp.broadcast_to(rounded, (16, TILE))
    direct = rounded.astype(F32)

    def slot_order(k):
        if not seam:
            return lax.rem(me_t + k + 1, links)
        block = links // 2
        near = jnp.where(k < 12, k - 4, jnp.where(k < 15, k - 11, 0))
        turn = jnp.where(k < block, k, near)
        side = me_t // block
        side = jnp.where(k < block, 1 - side, side)
        return side * block + lax.rem(me_t + turn, block)

    def slot_copy(k):
        peer = slot_order(k)
        return pltpu.make_async_remote_copy(
            src_ref=slot_send.at[peer],
            dst_ref=slot_recv.at[me_t],
            send_sem=slot_send_sems.at[k],
            recv_sem=slot_recv_sems.at[me_t],
            device_id={"link": peer},
            device_id_type=MESH,
        )

    @pl.loop(0, links)
    def _(k):
        peer = slot_order(k)
        at = pl.ds(pl.multiple_of(peer * pieces, HALF), pieces)
        values = []
        for c in range(slots):
            block = rows[c, at, :]
            if c % 2:
                value = block.astype(F32) * direct
                value = value[:, :HALF] + value[:, HALF:]
                values.append(jnp.sum(value.T, axis=0, keepdims=True))
            else:
                value = lax.dot_general(
                    half, block, (((1,), (1,)), ((), ())), preferred_element_type=F32
                )
                values.append(value[:1, :])
        values.append(jnp.zeros((16 - slots, pieces), F32))
        slot_send[peer] = jnp.concatenate(values, axis=0)

        @pl.when(k + 1 < links)
        def _():
            slot_copy(k).start()

    slot_recv[me_t] = slot_send[me_t]

    @pl.loop(1, links)
    def _(k):
        source = link_source(k)
        pltpu.make_async_remote_copy(
            src_ref=slot_send.at[source],
            dst_ref=slot_recv.at[source],
            send_sem=slot_send_sems.at[k],
            recv_sem=slot_recv_sems.at[source],
            device_id={"link": source},
            device_id_type=MESH,
        ).wait_recv()

    values = slot_recv[...].reshape(links * 16, pieces)
    summed = dot_tt(spread[...], values)
    columns = scaling[:, pl.ds(pl.multiple_of(me_t * pieces, HALF), pieces)]
    step_out[...] = columns * summed[:scen_count, :]

    @pl.loop(1, scens)
    def _(k):
        part_copy(k).wait_send()
        full_copy(k).wait_send()

    @pl.when(me_t + 1 < links)
    def _():
        up_copy.wait_send()

        @pl.loop(1, scens)
        def _(k):
            upart_copy(k).wait_send()
            ufull_copy(k).wait_send()

    @pl.when(me_t > 0)
    def _():
        down_copy.wait_send()

        @pl.loop(0, scens)
        def _(k):
            bpart_copy(k).wait_send()

    for step in range(2 * SWEEPS - 1):

        @pl.when(colour == step % 2)
        def _():
            @pl.when(me_t > 0)
            def _():
                vec_act(step, 0, lambda copy: copy.wait_send())

            @pl.when(me_t + 1 < links)
            def _():
                vec_act(step, 1, lambda copy: copy.wait_send())

    @pl.loop(0, links - 1)
    def _(k):
        slot_copy(k).wait_send()


def hand_over(direction, step, direction_out, step_out):
    direction_out[...] = direction[...]
    step_out[...] = step[...]


def shards(link_rows, slot_scenario, diag_scaling, regulariser, right_side):
    scens, links = lax.axis_size("scen"), lax.axis_size("link")
    slots, width, _ = link_rows.shape
    scen_count = diag_scaling.shape[0]
    pieces = width // links
    steps = 2 * SWEEPS - 1
    vmem = pl.BlockSpec(memory_space=pltpu.VMEM)
    dma = pltpu.SemaphoreType.DMA
    direction, step = pl.pallas_call(
        functools.partial(kernel, scens, links),
        out_shape=(
            pltpu.VMEM((1, TILE), F32),
            pltpu.VMEM((scen_count, pieces), F32),
        ),
        in_specs=[
            pl.BlockSpec(memory_space=pltpu.SMEM),
            vmem,
            pl.BlockSpec(memory_space=pl.ANY),
            pl.BlockSpec(memory_space=pl.ANY),
            vmem,
            vmem,
        ],
        out_specs=(vmem, vmem),
        scratch_shapes=[
            pltpu.VMEM((slots, width, TILE), BF16),
            pltpu.VMEM((scen_count, width), F32),
            pltpu.VMEM((TILE, TILE), F32),
            pltpu.VMEM((3 * HALF, HALF), F32),
            pltpu.VMEM((scens, 3 * HALF // scens, HALF), F32),
            pltpu.VMEM((3 * HALF, HALF), F32),
            pltpu.VMEM((TILE, TILE), F32),
            pltpu.VMEM((TILE, width // 2), BF16),
            pltpu.VMEM((PIECES, TILE, width // 2 // PIECES), BF16),
            pltpu.VMEM((PIECES, TILE, width // 2 // PIECES), BF16),
            pltpu.VMEM((width // 2, TILE), BF16),
            pltpu.VMEM((width // 2, TILE), BF16),
            pltpu.VMEM((2 * TILE, HALF), BF16),
            pltpu.VMEM((2 * TILE, HALF), BF16),
            pltpu.VMEM((2 * scens, 2 * TILE // scens, HALF), BF16),
            pltpu.VMEM((2 * TILE, HALF), BF16),
            pltpu.VMEM((1, TILE), F32),
            pltpu.VMEM((2 * steps, 8, HALF), F32),
            pltpu.VMEM((2 * steps, 8, HALF), F32),
            pltpu.VMEM((links * 16, TILE), F32),
            pltpu.VMEM((links, 16, pieces), F32),
            pltpu.VMEM((links, 16, pieces), F32),
            dma((slots,)),
            dma,
            dma((scens,)),
            dma((scens,)),
            dma((scens,)),
            dma((scens,)),
            dma((2,)),
            dma((2,)),
            dma((scens,)),
            dma((scens,)),
            dma((scens,)),
            dma((scens,)),
            dma((scens,)),
            dma((scens,)),
            dma((4 * steps,)),
            dma((2 * steps,)),
            dma((links,)),
            dma((links,)),
        ],
        compiler_params=pltpu.CompilerParams(
            collective_id=0, has_side_effects=True, vmem_limit_bytes=56 * 2**20
        ),
        name="coloured_sweeps",
    )(
        slot_scenario,
        slot_scenario,
        link_rows,
        diag_scaling,
        regulariser.reshape(1, TILE),
        right_side.reshape(1, TILE),
    )
    direction, step = pl.pallas_call(
        hand_over,
        out_shape=(
            jax.ShapeDtypeStruct((1, TILE), F32),
            jax.ShapeDtypeStruct((scen_count, pieces), F32),
        ),
        in_specs=[vmem, vmem],
        out_specs=(vmem, vmem),
        compiler_params=pltpu.CompilerParams(vmem_limit_bytes=2**20),
        name="hand_over",
    )(direction, step)
    return direction.reshape(TILE), step


def solution(mesh):
    in_specs = (P("scen", None, "link"), P("scen", None), P("scen", None), P("link"), P("link"))
    out_specs = (P("link"), P("scen", "link"))
    return jax.shard_map(shards, mesh=mesh, in_specs=in_specs, out_specs=out_specs, check_vma=False)
```

```python
import functools

import jax
import jax.numpy as jnp
from jax import lax
from jax.experimental import pallas as pl
from jax.experimental.pallas import tpu as pltpu
from jax.sharding import PartitionSpec as P

SWEEPS = 2
HALF = 128
AHEAD = 3
PIECES = 8
BELOW_TURN, UPPER_TURN = 2, 4
FIRST, SECOND = 2, 4
TILE = 256
PANEL = 32
HIGHEST = lax.Precision.HIGHEST
MESH = pl.DeviceIdType.MESH
BF16 = jnp.bfloat16
F32 = jnp.float32


def dot_tt(left, right):
    return lax.dot_general(
        left, right, (((0,), (0,)), ((), ())), precision=HIGHEST, preferred_element_type=F32
    )


def tree_sum(terms):
    while len(terms) > 1:
        pairs = [terms[i] + terms[i + 1] for i in range(0, len(terms) - 1, 2)]
        terms = pairs + terms[len(terms) - len(terms) % 2 :]
    return terms[0]


def pair_sweep(held, count, first):
    second = first + 1

    def get(i, j):
        return held[(min(i, j), max(i, j))]

    a, b, c = get(first, first), get(first, second), get(second, second)
    scale = 1.0 / (a * c - b * b)
    inv_a, inv_b, inv_c = c * scale, -(b * scale), a * scale
    others = [i for i in range(count) if i not in (first, second)]
    row0 = {i: inv_a * get(first, i) + inv_b * get(second, i) for i in others}
    row1 = {i: inv_b * get(first, i) + inv_c * get(second, i) for i in others}
    new = {}
    for at, i in enumerate(others):
        for j in others[at:]:
            new[(i, j)] = get(i, j) - (get(first, i) * row0[j] + get(second, i) * row1[j])
        new[(min(i, first), max(i, first))] = row0[i]
        new[(min(i, second), max(i, second))] = row1[i]
    new[(first, first)] = -inv_a
    new[(first, second)] = -inv_b
    new[(second, second)] = -inv_c
    return new


def panel_sweep(panel, start):
    rows, width = panel.shape
    lane = lax.broadcasted_iota(jnp.int32, (1, width), 1)
    sub = lax.broadcasted_iota(jnp.int32, (8, 1), 0)

    def wide(v):
        return jnp.concatenate([v] * (width // HALF), axis=1)

    for top in range(0, rows, 8):
        at = start + top
        own = panel[top : top + 8, :]
        columns = [panel[:, at + j : at + j + 1] for j in range(8)]
        held = {}
        for j in range(8):
            spread = jnp.broadcast_to(columns[j][top : top + 8], (8, HALF))
            for i in range(j + 1):
                held[(i, j)] = jnp.broadcast_to(spread[i : i + 1], (8, HALF))
        for first in range(0, 8, 2):
            held = pair_sweep(held, 8, first)
        inverse = []
        for j in range(8):
            column = held[(0, j)]
            for i in range(1, 8):
                column = jnp.where(sub == i, held[(min(i, j), max(i, j))], column)
            inverse.append(column)
        swept = -tree_sum([wide(inverse[j]) * own[j : j + 1, :] for j in range(8)])
        for j in range(8):
            swept = jnp.where(lane == at + j, wide(inverse[j]), swept)
        inside = (lane >= at) & (lane < at + 8)
        rest = jnp.where(inside, 0.0, panel) - tree_sum(
            [columns[j] * swept[j : j + 1, :] for j in range(8)]
        )
        parts = [rest[:top]] if top else []
        parts.append(swept)
        if top + 8 < rows:
            parts.append(rest[top + 8 :])
        panel = jnp.concatenate(parts, axis=0)
    return panel


def sweep_rows(matrix, start):
    before = matrix[start : start + PANEL, :]
    after = panel_sweep(before, start)
    lane = lax.broadcasted_iota(jnp.int32, (1, TILE), 1)
    inside = (lane >= start) & (lane < start + PANEL)
    matrix[...] = jnp.where(inside, 0.0, matrix[...]) - dot_tt(before, after)
    matrix[start : start + PANEL, :] = after


def kernel(
    scens,
    links,
    ids_s,
    ids_v,
    rows_hbm,
    scaling_hbm,
    regulariser,
    right_side,
    direction_out,
    step_out,
    rows,
    scaling,
    total,
    part,
    gathered,
    full,
    matrix,
    up_keep,
    up_send,
    up_got,
    down_send,
    down_got,
    upper_part,
    below_part,
    upper_gathered,
    upper_full,
    current,
    vec_send,
    vec_recv,
    spread,
    slot_send,
    slot_recv,
    row_sems,
    scaling_sem,
    part_send,
    part_recv,
    full_send,
    full_recv,
    up_sems,
    down_sems,
    upart_send,
    upart_recv,
    bpart_send,
    bpart_recv,
    ufull_send,
    ufull_recv,
    vsend_sems,
    vrecv_sems,
    slot_send_sems,
    slot_recv_sems,
):
    me_s = lax.axis_index("scen")
    me_t = lax.axis_index("link")
    slots, width, _ = rows.shape
    scen_count = scaling.shape[0]
    pieces = width // links
    chunk = part.shape[0] // scens
    uchunk = upper_part.shape[0] // scens

    def scen_peer(k):
        return lax.rem(me_s + k, scens)

    def scen_source(k):
        return lax.rem(me_s + scens - k, scens)

    def link_peer(k):
        return lax.rem(me_t + k, links)

    def link_source(k):
        return lax.rem(me_t + links - k, links)

    scaling_copy = pltpu.make_async_copy(scaling_hbm, scaling, scaling_sem)
    scaling_copy.start()

    def row_copy(c):
        return pltpu.make_async_copy(rows_hbm.at[c], rows.at[c], row_sems.at[c])

    for c in range(AHEAD):
        row_copy(c).start()

    vec_recv[...] = jnp.zeros_like(vec_recv)
    barrier = pltpu.get_barrier_semaphore()

    def greet(scen, link):
        pl.semaphore_signal(
            barrier, 1, device_id={"scen": scen, "link": link}, device_id_type=MESH
        )

    @pl.loop(1, scens)
    def _(k):
        greet(scen_peer(k), me_t)
        greet(scen_peer(k), link_peer(1))
        greet(scen_peer(k), link_source(1))

    @pl.loop(1, links)
    def _(k):
        greet(me_s, link_peer(k))

    next_t = jnp.minimum(me_t + 1, links - 1)
    prev_t = jnp.maximum(me_t - 1, 0)
    here = [ids_s[c, me_t] for c in range(slots)]
    after = [ids_s[c, next_t] for c in range(slots)]
    before = [ids_s[c, prev_t] for c in range(slots)]
    up_slot, up_found, down_slot = jnp.int32(0), jnp.int32(0), jnp.int32(0)
    for c in range(slots):
        up_hit, down_hit = jnp.int32(0), jnp.int32(0)
        for other in range(slots):
            up_hit = up_hit | (here[c] == after[other]).astype(jnp.int32)
            down_hit = down_hit | (here[c] == before[other]).astype(jnp.int32)
        live = (here[c] < scen_count).astype(jnp.int32)
        up_hit = up_hit * live
        down_hit = down_hit * live
        up_slot = jnp.where(up_hit > 0, c, up_slot)
        up_found = up_found | up_hit
        down_slot = jnp.where(down_hit > 0, c, down_slot)
    up_found = jnp.where(me_t + 1 < links, up_found, 0)

    spread[...] = jnp.zeros_like(spread)
    names = lax.broadcasted_iota(jnp.int32, (slots, TILE), 1)
    for t in range(links):
        spread[t * 16 : t * 16 + slots, :] = (ids_v[:, t : t + 1] == names).astype(F32)

    def scale_row(name, keep):
        row = scaling[pl.ds(jnp.minimum(name, scen_count - 1), 1), :]
        return row * keep.astype(F32)

    total[...] = jnp.zeros_like(total)
    scaling_copy.wait()

    def add_slot(c):
        name = ids_s[c, me_t]
        row = scale_row(name, (name < scen_count).astype(jnp.int32))
        terms = []
        for at in range(0, width, TILE):
            block = rows[c, at : at + TILE, :]
            scaled = (block.T.astype(F32) * row[:, at : at + TILE]).astype(BF16)
            terms.append(jnp.dot(scaled, block, preferred_element_type=F32))
        summed = terms[0]
        for term in terms[1:]:
            summed = summed + term
        total[...] += summed

    def arrived(c):
        row_copy(c).wait()

        @pl.when(c + AHEAD < slots)
        def _():
            row_copy(c + AHEAD).start()

    early = slots - AHEAD

    @pl.loop(0, early)
    def _(c):
        arrived(c)
        add_slot(c)

    @pl.loop(early, slots)
    def _(c):
        arrived(c)

    part_width = width // 2
    up_row = scale_row(ids_s[up_slot, me_t], up_found)
    for at in range(0, part_width, TILE):
        down_send[at : at + TILE, :] = rows[down_slot, at : at + TILE, :]
    for at in range(0, part_width, TILE):
        beyond = part_width + at
        block = rows[up_slot, beyond : beyond + TILE, :]
        scaled = (block.T.astype(F32) * up_row[:, beyond : beyond + TILE]).astype(BF16)
        for inner in range(0, TILE, part_width // PIECES):
            up_send[(at + inner) // (part_width // PIECES)] = scaled[
                :, inner : inner + part_width // PIECES
            ]

    pl.semaphore_wait(barrier, 3 * (scens - 1) + links - 1)

    piece = part_width // PIECES
    seam = scens == 16 and links == 16

    def at_seam(side):
        return (me_t == links // 2 - side) if seam else (me_t < 0)

    def row_pieces(side, at, count):
        if side == 0:
            span = pl.ds(at * piece, count * piece)
            source, target = down_send.at[span], down_got.at[span]
            sems, peer = down_sems, link_source(1)
        else:
            span = pl.ds(at, count)
            source, target = up_send.at[span], up_got.at[span]
            sems, peer = up_sems, link_peer(1)
        return pltpu.make_async_remote_copy(
            src_ref=source,
            dst_ref=target,
            send_sem=sems.at[0],
            recv_sem=sems.at[1],
            device_id={"link": peer},
            device_id_type=MESH,
        )

    down_copy = row_pieces(0, 0, PIECES)
    up_copy = row_pieces(1, 0, PIECES)

    def seam_rows(first, last):
        for side in range(2):

            @pl.when(at_seam(side))
            def _():
                for at in range(first, last):
                    row_pieces(side, at, 1).start()

    @pl.when((me_t > 0) & jnp.logical_not(at_seam(0)))
    def _():
        down_copy.start()

    @pl.when((me_t + 1 < links) & jnp.logical_not(at_seam(1)))
    def _():
        up_copy.start()

    if seam:
        seam_rows(0, FIRST)

    for at in range(0, part_width, TILE):
        block = rows[up_slot, at : at + TILE, :]
        up_keep[:, at : at + TILE] = (
            block.T.astype(F32) * up_row[:, at : at + TILE]
        ).astype(BF16)

    @pl.loop(early, slots)
    def _(c):
        add_slot(c)

    low, high = total[:HALF, :HALF], total[HALF:, HALF:]
    part[:HALF, :] = 0.5 * (low + low.T)
    part[HALF : 2 * HALF, :] = 0.5 * (total[HALF:, :HALF] + total[:HALF, HALF:].T)
    part[2 * HALF :, :] = 0.5 * (high + high.T)

    def part_copy(k):
        peer = scen_peer(k)
        return pltpu.make_async_remote_copy(
            src_ref=part.at[pl.ds(pl.multiple_of(peer * chunk, 8), chunk)],
            dst_ref=gathered.at[me_s],
            send_sem=part_send.at[k],
            recv_sem=part_recv.at[me_s],
            device_id={"scen": peer},
            device_id_type=MESH,
        )

    def part_wait(k):
        source = scen_source(k)
        pltpu.make_async_remote_copy(
            src_ref=part.at[pl.ds(0, chunk)],
            dst_ref=gathered.at[source],
            send_sem=part_send.at[k],
            recv_sem=part_recv.at[source],
            device_id={"scen": source},
            device_id_type=MESH,
        ).wait_recv()

    def full_copy(k):
        mine = pl.ds(pl.multiple_of(me_s * chunk, 8), chunk)
        return pltpu.make_async_remote_copy(
            src_ref=full.at[mine],
            dst_ref=full.at[mine],
            send_sem=full_send.at[k],
            recv_sem=full_recv.at[me_s],
            device_id={"scen": scen_peer(k)},
            device_id_type=MESH,
        )

    def full_wait(k):
        source = scen_source(k)
        theirs = pl.ds(pl.multiple_of(source * chunk, 8), chunk)
        pltpu.make_async_remote_copy(
            src_ref=full.at[theirs],
            dst_ref=full.at[theirs],
            send_sem=full_send.at[k],
            recv_sem=full_recv.at[source],
            device_id={"scen": source},
            device_id_type=MESH,
        ).wait_recv()

    def upart_copy(k):
        peer = scen_peer(k)
        return pltpu.make_async_remote_copy(
            src_ref=upper_part.at[pl.ds(pl.multiple_of(peer * uchunk, 16), uchunk)],
            dst_ref=upper_gathered.at[me_s],
            send_sem=upart_send.at[k],
            recv_sem=upart_recv.at[me_s],
            device_id={"scen": peer},
            device_id_type=MESH,
        )

    def upart_wait(k):
        source = scen_source(k)
        pltpu.make_async_remote_copy(
            src_ref=upper_part.at[pl.ds(0, uchunk)],
            dst_ref=upper_gathered.at[source],
            send_sem=upart_send.at[k],
            recv_sem=upart_recv.at[source],
            device_id={"scen": source},
            device_id_type=MESH,
        ).wait_recv()

    def bpart_copy(k):
        peer = scen_peer(k)
        return pltpu.make_async_remote_copy(
            src_ref=below_part.at[pl.ds(pl.multiple_of(peer * uchunk, 16), uchunk)],
            dst_ref=upper_gathered.at[scens + me_s],
            send_sem=bpart_send.at[k],
            recv_sem=bpart_recv.at[me_s],
            device_id={"scen": peer, "link": link_source(1)},
            device_id_type=MESH,
        )

    def bpart_wait(k):
        source = scen_source(k)
        pltpu.make_async_remote_copy(
            src_ref=below_part.at[pl.ds(0, uchunk)],
            dst_ref=upper_gathered.at[scens + source],
            send_sem=bpart_send.at[k],
            recv_sem=bpart_recv.at[source],
            device_id={"scen": source, "link": link_peer(1)},
            device_id_type=MESH,
        ).wait_recv()

    def ufull_copy(k):
        mine = pl.ds(pl.multiple_of(me_s * uchunk, 16), uchunk)
        return pltpu.make_async_remote_copy(
            src_ref=upper_full.at[mine],
            dst_ref=upper_full.at[mine],
            send_sem=ufull_send.at[k],
            recv_sem=ufull_recv.at[me_s],
            device_id={"scen": scen_peer(k)},
            device_id_type=MESH,
        )

    def ufull_wait(k):
        source = scen_source(k)
        theirs = pl.ds(pl.multiple_of(source * uchunk, 16), uchunk)
        pltpu.make_async_remote_copy(
            src_ref=upper_full.at[theirs],
            dst_ref=upper_full.at[theirs],
            send_sem=ufull_send.at[k],
            recv_sem=ufull_recv.at[source],
            device_id={"scen": source},
            device_id_type=MESH,
        ).wait_recv()

    @pl.loop(1, scens)
    def _(k):
        part_copy(k).start()

    if seam:
        seam_rows(FIRST, SECOND)

    gathered[me_s] = part[pl.ds(pl.multiple_of(me_s * chunk, 8), chunk), :]

    @pl.loop(1, scens)
    def _(k):
        part_wait(k)

    full[pl.ds(pl.multiple_of(me_s * chunk, 8), chunk), :] = tree_sum(
        [gathered[i] for i in range(scens)]
    )

    @pl.loop(1, scens)
    def _(k):
        full_copy(k).start()

    if seam:
        seam_rows(SECOND, PIECES)

    @pl.loop(1, scens)
    def _(k):
        full_wait(k)

    corner = full[HALF : 2 * HALF, :]
    matrix[:HALF, :HALF] = full[:HALF, :]
    matrix[HALF:, :HALF] = corner
    matrix[:HALF, HALF:] = corner.T
    matrix[HALF:, HALF:] = full[2 * HALF :, :]
    on_diag = lax.broadcasted_iota(jnp.int32, (TILE, TILE), 0) == lax.broadcasted_iota(
        jnp.int32, (TILE, TILE), 1
    )
    matrix[...] += jnp.where(on_diag, regulariser[...], 0.0)

    def store_wide(ref, value):
        ref[:TILE, :] = value[:, :HALF].astype(BF16)
        ref[TILE:, :] = value[:, HALF:].astype(BF16)

    def below_terms():
        @pl.when(me_t > 0)
        def _():
            up_copy.wait_recv()
            scaled = jnp.concatenate([up_got[i] for i in range(PIECES)], axis=1)
            store_wide(
                below_part,
                jnp.dot(scaled, rows[down_slot, part_width:, :], preferred_element_type=F32),
            )

            @pl.loop(0, scens)
            def _(k):
                bpart_copy(k).start()

    def upper_terms():
        @pl.when(me_t + 1 < links)
        def _():
            down_copy.wait_recv()
            store_wide(
                upper_part,
                jnp.dot(up_keep[...], down_got[...], preferred_element_type=F32),
            )

            @pl.loop(1, scens)
            def _(k):
                upart_copy(k).start()

            upper_gathered[me_s] = upper_part[
                pl.ds(pl.multiple_of(me_s * uchunk, 16), uchunk), :
            ]

    def upper_sum():
        @pl.when(me_t + 1 < links)
        def _():
            @pl.loop(1, scens)
            def _(k):
                upart_wait(k)

            @pl.loop(0, scens)
            def _(k):
                bpart_wait(k)

            upper_full[pl.ds(pl.multiple_of(me_s * uchunk, 16), uchunk), :] = tree_sum(
                [upper_gathered[i].astype(F32) for i in range(2 * scens)]
            ).astype(BF16)

            @pl.loop(1, scens)
            def _(k):
                ufull_copy(k).start()

    for at in range(0, TILE, PANEL):
        sweep_rows(matrix, at)
        turn = at // PANEL
        if turn == 0:
            pl.when(jnp.logical_not(at_seam(0)))(below_terms)
            pl.when(jnp.logical_not(at_seam(1)))(upper_terms)
        if seam and turn == BELOW_TURN:
            pl.when(at_seam(0))(below_terms)
        if seam and turn == UPPER_TURN:
            pl.when(at_seam(1))(upper_terms)
        if at == 4 * PANEL:
            pl.when(jnp.logical_not(at_seam(1)))(upper_sum)

    if seam:
        pl.when(at_seam(1))(upper_sum)

    def solve(vector):
        wide = jnp.broadcast_to(vector, (8, TILE))
        found = -jnp.dot(wide, matrix[...], precision=HIGHEST, preferred_element_type=F32)
        return found[:1, :]

    def split(vector):
        first = vector.astype(BF16)
        left = vector - first.astype(F32)
        second = left.astype(BF16)
        third = (left - second.astype(F32)).astype(BF16)
        parts = [jnp.broadcast_to(v.astype(F32), (8, TILE)) for v in (first, second, third)]
        sub = lax.broadcasted_iota(jnp.int32, (8, TILE), 0)
        mixed = jnp.where(sub == 0, parts[0], jnp.where(sub == 1, parts[1], parts[2]))
        return jnp.where(sub < 3, mixed, 0.0).astype(BF16)

    def to_next(vector):
        parts = split(vector)
        low = jnp.dot(parts, upper_full[:TILE, :], preferred_element_type=F32)
        high = jnp.dot(parts, upper_full[TILE:, :], preferred_element_type=F32)
        return jnp.sum(jnp.concatenate([low, high], axis=1), axis=0, keepdims=True)

    def from_next(vector):
        parts = split(vector)
        turned = (((1,), (1,)), ((), ()))
        low = lax.dot_general(
            parts[:, :HALF], upper_full[:TILE, :], turned, preferred_element_type=F32
        )
        high = lax.dot_general(
            parts[:, HALF:], upper_full[TILE:, :], turned, preferred_element_type=F32
        )
        return jnp.sum(low + high, axis=0, keepdims=True)

    def put(ref, vector):
        ref[0:1, :] = vector[:, :HALF]
        ref[1:2, :] = vector[:, HALF:]

    def fetch(ref):
        return jnp.concatenate([ref[0:1, :], ref[1:2, :]], axis=1)

    lane_count = 4
    lane = lax.rem(me_s, lane_count)
    first_lane = me_s - lane

    def vec_copy(step, side, extra):
        cross = at_seam(side)
        if extra:
            target = first_lane + jnp.where(lane == 0, 2, 1)
        else:
            target = jnp.where(cross, first_lane + lane_count - 1 - lane, me_s)
        slot = 2 * step + side
        return pltpu.make_async_remote_copy(
            src_ref=vec_send.at[slot],
            dst_ref=vec_recv.at[slot],
            send_sem=vsend_sems.at[2 * slot + extra],
            recv_sem=vrecv_sems.at[slot],
            device_id={
                "scen": target,
                "link": link_source(1) if side == 0 else link_peer(1),
            },
            device_id_type=MESH,
        )

    def vec_act(step, side, act):
        cross = at_seam(side)
        edge = (lane == 0) | (lane == lane_count - 1)

        @pl.when(jnp.logical_not(cross) | edge)
        def _():
            act(vec_copy(step, side, 0))

        if seam:

            @pl.when(cross & edge)
            def _():
                act(vec_copy(step, side, 1))

    colour = lax.rem(me_t, 2)
    vec_send[...] = jnp.zeros_like(vec_send)
    current[...] = jnp.zeros_like(current)

    @pl.when(colour == 0)
    def _():
        current[...] = solve(right_side[...])

    @pl.when(me_t + 1 < links)
    def _():
        @pl.loop(1, scens)
        def _(k):
            ufull_wait(k)

    for step in range(2 * SWEEPS - 1):

        @pl.when(colour == step % 2)
        def _():
            @pl.when(me_t > 0)
            def _():
                put(vec_send.at[2 * step], current[...])
                vec_act(step, 0, lambda copy: copy.start())

            @pl.when(me_t + 1 < links)
            def _():
                put(vec_send.at[2 * step + 1], to_next(current[...]))
                vec_act(step, 1, lambda copy: copy.start())

        @pl.when(colour != step % 2)
        def _():
            current[...] = right_side[...]

            @pl.when(me_t + 1 < links)
            def _():
                vec_copy(step, 0, 0).wait_recv()
                current[...] -= from_next(fetch(vec_recv.at[2 * step]))

            @pl.when(me_t > 0)
            def _():
                vec_copy(step, 1, 0).wait_recv()
                current[...] -= fetch(vec_recv.at[2 * step + 1])

            current[...] = solve(current[...])

    direction_out[...] = current[...]

    rounded = current[...].astype(BF16)
    half = jnp.broadcast_to(rounded, (16, TILE))
    direct = rounded.astype(F32)

    def slot_order(k):
        if not seam:
            return lax.rem(me_t + k + 1, links)
        block = links // 2
        near = jnp.where(k < 12, k - 4, jnp.where(k < 15, k - 11, 0))
        turn = jnp.where(k < block, k, near)
        side = me_t // block
        side = jnp.where(k < block, 1 - side, side)
        return side * block + lax.rem(me_t + turn, block)

    def slot_copy(k):
        peer = slot_order(k)
        return pltpu.make_async_remote_copy(
            src_ref=slot_send.at[peer],
            dst_ref=slot_recv.at[me_t],
            send_sem=slot_send_sems.at[k],
            recv_sem=slot_recv_sems.at[me_t],
            device_id={"link": peer},
            device_id_type=MESH,
        )

    @pl.loop(0, links)
    def _(k):
        peer = slot_order(k)
        at = pl.ds(pl.multiple_of(peer * pieces, HALF), pieces)
        values = []
        for c in range(slots):
            block = rows[c, at, :]
            if c % 2:
                value = block.astype(F32) * direct
                value = value[:, :HALF] + value[:, HALF:]
                values.append(jnp.sum(value.T, axis=0, keepdims=True))
            else:
                value = lax.dot_general(
                    half, block, (((1,), (1,)), ((), ())), preferred_element_type=F32
                )
                values.append(value[:1, :])
        values.append(jnp.zeros((16 - slots, pieces), F32))
        slot_send[peer] = jnp.concatenate(values, axis=0)

        @pl.when(k + 1 < links)
        def _():
            slot_copy(k).start()

    slot_recv[me_t] = slot_send[me_t]

    @pl.loop(1, links)
    def _(k):
        source = link_source(k)
        pltpu.make_async_remote_copy(
            src_ref=slot_send.at[source],
            dst_ref=slot_recv.at[source],
            send_sem=slot_send_sems.at[k],
            recv_sem=slot_recv_sems.at[source],
            device_id={"link": source},
            device_id_type=MESH,
        ).wait_recv()

    values = slot_recv[...].reshape(links * 16, pieces)
    summed = dot_tt(spread[...], values)
    columns = scaling[:, pl.ds(pl.multiple_of(me_t * pieces, HALF), pieces)]
    step_out[...] = columns * summed[:scen_count, :]

    @pl.loop(1, scens)
    def _(k):
        part_copy(k).wait_send()
        full_copy(k).wait_send()

    @pl.when(me_t + 1 < links)
    def _():
        up_copy.wait_send()

        @pl.loop(1, scens)
        def _(k):
            upart_copy(k).wait_send()
            ufull_copy(k).wait_send()

    @pl.when(me_t > 0)
    def _():
        down_copy.wait_send()

        @pl.loop(0, scens)
        def _(k):
            bpart_copy(k).wait_send()

    for step in range(2 * SWEEPS - 1):

        @pl.when(colour == step % 2)
        def _():
            @pl.when(me_t > 0)
            def _():
                vec_act(step, 0, lambda copy: copy.wait_send())

            @pl.when(me_t + 1 < links)
            def _():
                vec_act(step, 1, lambda copy: copy.wait_send())

    @pl.loop(0, links - 1)
    def _(k):
        slot_copy(k).wait_send()


def hand_over(direction, step, direction_out, step_out):
    direction_out[...] = direction[...]
    step_out[...] = step[...]


def shards(link_rows, slot_scenario, diag_scaling, regulariser, right_side):
    scens, links = lax.axis_size("scen"), lax.axis_size("link")
    slots, width, _ = link_rows.shape
    scen_count = diag_scaling.shape[0]
    pieces = width // links
    steps = 2 * SWEEPS - 1
    vmem = pl.BlockSpec(memory_space=pltpu.VMEM)
    dma = pltpu.SemaphoreType.DMA
    direction, step = pl.pallas_call(
        functools.partial(kernel, scens, links),
        out_shape=(
            pltpu.VMEM((1, TILE), F32),
            pltpu.VMEM((scen_count, pieces), F32),
        ),
        in_specs=[
            pl.BlockSpec(memory_space=pltpu.SMEM),
            vmem,
            pl.BlockSpec(memory_space=pl.ANY),
            pl.BlockSpec(memory_space=pl.ANY),
            vmem,
            vmem,
        ],
        out_specs=(vmem, vmem),
        scratch_shapes=[
            pltpu.VMEM((slots, width, TILE), BF16),
            pltpu.VMEM((scen_count, width), F32),
            pltpu.VMEM((TILE, TILE), F32),
            pltpu.VMEM((3 * HALF, HALF), F32),
            pltpu.VMEM((scens, 3 * HALF // scens, HALF), F32),
            pltpu.VMEM((3 * HALF, HALF), F32),
            pltpu.VMEM((TILE, TILE), F32),
            pltpu.VMEM((TILE, width // 2), BF16),
            pltpu.VMEM((PIECES, TILE, width // 2 // PIECES), BF16),
            pltpu.VMEM((PIECES, TILE, width // 2 // PIECES), BF16),
            pltpu.VMEM((width // 2, TILE), BF16),
            pltpu.VMEM((width // 2, TILE), BF16),
            pltpu.VMEM((2 * TILE, HALF), BF16),
            pltpu.VMEM((2 * TILE, HALF), BF16),
            pltpu.VMEM((2 * scens, 2 * TILE // scens, HALF), BF16),
            pltpu.VMEM((2 * TILE, HALF), BF16),
            pltpu.VMEM((1, TILE), F32),
            pltpu.VMEM((2 * steps, 8, HALF), F32),
            pltpu.VMEM((2 * steps, 8, HALF), F32),
            pltpu.VMEM((links * 16, TILE), F32),
            pltpu.VMEM((links, 16, pieces), F32),
            pltpu.VMEM((links, 16, pieces), F32),
            dma((slots,)),
            dma,
            dma((scens,)),
            dma((scens,)),
            dma((scens,)),
            dma((scens,)),
            dma((2,)),
            dma((2,)),
            dma((scens,)),
            dma((scens,)),
            dma((scens,)),
            dma((scens,)),
            dma((scens,)),
            dma((scens,)),
            dma((4 * steps,)),
            dma((2 * steps,)),
            dma((links,)),
            dma((links,)),
        ],
        compiler_params=pltpu.CompilerParams(
            collective_id=0, has_side_effects=True, vmem_limit_bytes=56 * 2**20
        ),
        name="coloured_sweeps",
    )(
        slot_scenario,
        slot_scenario,
        link_rows,
        diag_scaling,
        regulariser.reshape(1, TILE),
        right_side.reshape(1, TILE),
    )
    direction, step = pl.pallas_call(
        hand_over,
        out_shape=(
            jax.ShapeDtypeStruct((1, TILE), F32),
            jax.ShapeDtypeStruct((scen_count, pieces), F32),
        ),
        in_specs=[vmem, vmem],
        out_specs=(vmem, vmem),
        compiler_params=pltpu.CompilerParams(vmem_limit_bytes=2**20),
        name="hand_over",
    )(direction, step)
    return direction.reshape(TILE), step


def solution(mesh):
    in_specs = (P("scen", None, "link"), P("scen", None), P("scen", None), P("link"), P("link"))
    out_specs = (P("link"), P("scen", "link"))
    return jax.shard_map(shards, mesh=mesh, in_specs=in_specs, out_specs=out_specs, check_vma=False)
```

```python
import functools

import jax
import jax.numpy as jnp
from jax import lax
from jax.experimental import pallas as pl
from jax.experimental.pallas import tpu as pltpu
from jax.sharding import PartitionSpec as P

SWEEPS = 2
HALF = 128
AHEAD = 3
PIECES = 8
BELOW_TURN, UPPER_TURN = 2, 4
FIRST, SECOND = 2, 4
TILE = 256
PANEL = 32
HIGHEST = lax.Precision.HIGHEST
MESH = pl.DeviceIdType.MESH
BF16 = jnp.bfloat16
F32 = jnp.float32


def dot_tt(left, right):
    return lax.dot_general(
        left, right, (((0,), (0,)), ((), ())), precision=HIGHEST, preferred_element_type=F32
    )


def tree_sum(terms):
    while len(terms) > 1:
        pairs = [terms[i] + terms[i + 1] for i in range(0, len(terms) - 1, 2)]
        terms = pairs + terms[len(terms) - len(terms) % 2 :]
    return terms[0]


def pair_sweep(held, count, first):
    second = first + 1

    def get(i, j):
        return held[(min(i, j), max(i, j))]

    a, b, c = get(first, first), get(first, second), get(second, second)
    scale = 1.0 / (a * c - b * b)
    inv_a, inv_b, inv_c = c * scale, -(b * scale), a * scale
    others = [i for i in range(count) if i not in (first, second)]
    row0 = {i: inv_a * get(first, i) + inv_b * get(second, i) for i in others}
    row1 = {i: inv_b * get(first, i) + inv_c * get(second, i) for i in others}
    new = {}
    for at, i in enumerate(others):
        for j in others[at:]:
            new[(i, j)] = get(i, j) - (get(first, i) * row0[j] + get(second, i) * row1[j])
        new[(min(i, first), max(i, first))] = row0[i]
        new[(min(i, second), max(i, second))] = row1[i]
    new[(first, first)] = -inv_a
    new[(first, second)] = -inv_b
    new[(second, second)] = -inv_c
    return new


def panel_sweep(panel, start):
    rows, width = panel.shape
    lane = lax.broadcasted_iota(jnp.int32, (1, width), 1)
    sub = lax.broadcasted_iota(jnp.int32, (8, 1), 0)

    def wide(v):
        return jnp.concatenate([v] * (width // HALF), axis=1)

    for top in range(0, rows, 8):
        at = start + top
        own = panel[top : top + 8, :]
        columns = [panel[:, at + j : at + j + 1] for j in range(8)]
        held = {}
        for j in range(8):
            spread = jnp.broadcast_to(columns[j][top : top + 8], (8, HALF))
            for i in range(j + 1):
                held[(i, j)] = jnp.broadcast_to(spread[i : i + 1], (8, HALF))
        for first in range(0, 8, 2):
            held = pair_sweep(held, 8, first)
        inverse = []
        for j in range(8):
            column = held[(0, j)]
            for i in range(1, 8):
                column = jnp.where(sub == i, held[(min(i, j), max(i, j))], column)
            inverse.append(column)
        swept = -tree_sum([wide(inverse[j]) * own[j : j + 1, :] for j in range(8)])
        for j in range(8):
            swept = jnp.where(lane == at + j, wide(inverse[j]), swept)
        inside = (lane >= at) & (lane < at + 8)
        rest = jnp.where(inside, 0.0, panel) - tree_sum(
            [columns[j] * swept[j : j + 1, :] for j in range(8)]
        )
        parts = [rest[:top]] if top else []
        parts.append(swept)
        if top + 8 < rows:
            parts.append(rest[top + 8 :])
        panel = jnp.concatenate(parts, axis=0)
    return panel


def sweep_rows(matrix, start):
    before = matrix[start : start + PANEL, :]
    after = panel_sweep(before, start)
    lane = lax.broadcasted_iota(jnp.int32, (1, TILE), 1)
    inside = (lane >= start) & (lane < start + PANEL)
    matrix[...] = jnp.where(inside, 0.0, matrix[...]) - dot_tt(before, after)
    matrix[start : start + PANEL, :] = after


def kernel(
    scens,
    links,
    ids_s,
    ids_v,
    rows_hbm,
    scaling_hbm,
    regulariser,
    right_side,
    direction_out,
    step_out,
    rows,
    scaling,
    total,
    part,
    gathered,
    full,
    matrix,
    up_keep,
    up_send,
    up_got,
    down_send,
    down_got,
    upper_part,
    below_part,
    upper_gathered,
    upper_full,
    current,
    vec_send,
    vec_recv,
    spread,
    slot_send,
    slot_recv,
    row_sems,
    scaling_sem,
    part_send,
    part_recv,
    full_send,
    full_recv,
    up_sems,
    down_sems,
    upart_send,
    upart_recv,
    bpart_send,
    bpart_recv,
    ufull_send,
    ufull_recv,
    vsend_sems,
    vrecv_sems,
    slot_send_sems,
    slot_recv_sems,
):
    me_s = lax.axis_index("scen")
    me_t = lax.axis_index("link")
    slots, width, _ = rows.shape
    scen_count = scaling.shape[0]
    pieces = width // links
    chunk = part.shape[0] // scens
    uchunk = upper_part.shape[0] // scens

    def scen_peer(k):
        return lax.rem(me_s + k, scens)

    def link_peer(k):
        return lax.rem(me_t + k, links)

    def link_source(k):
        return lax.rem(me_t + links - k, links)

    scaling_copy = pltpu.make_async_copy(scaling_hbm, scaling, scaling_sem)
    scaling_copy.start()

    def row_copy(c):
        return pltpu.make_async_copy(rows_hbm.at[c], rows.at[c], row_sems.at[c])

    for c in range(AHEAD):
        row_copy(c).start()

    vec_recv[...] = jnp.zeros_like(vec_recv)
    barrier = pltpu.get_barrier_semaphore()

    def greet(scen, link):
        pl.semaphore_signal(
            barrier, 1, device_id={"scen": scen, "link": link}, device_id_type=MESH
        )

    @pl.loop(1, scens)
    def _(k):
        greet(scen_peer(k), me_t)
        greet(scen_peer(k), link_peer(1))
        greet(scen_peer(k), link_source(1))

    @pl.loop(1, links)
    def _(k):
        greet(me_s, link_peer(k))

    next_t = jnp.minimum(me_t + 1, links - 1)
    prev_t = jnp.maximum(me_t - 1, 0)
    here = [ids_s[c, me_t] for c in range(slots)]
    after = [ids_s[c, next_t] for c in range(slots)]
    before = [ids_s[c, prev_t] for c in range(slots)]
    up_slot, up_found, down_slot = jnp.int32(0), jnp.int32(0), jnp.int32(0)
    for c in range(slots):
        up_hit, down_hit = jnp.int32(0), jnp.int32(0)
        for other in range(slots):
            up_hit = up_hit | (here[c] == after[other]).astype(jnp.int32)
            down_hit = down_hit | (here[c] == before[other]).astype(jnp.int32)
        live = (here[c] < scen_count).astype(jnp.int32)
        up_hit = up_hit * live
        down_hit = down_hit * live
        up_slot = jnp.where(up_hit > 0, c, up_slot)
        up_found = up_found | up_hit
        down_slot = jnp.where(down_hit > 0, c, down_slot)
    up_found = jnp.where(me_t + 1 < links, up_found, 0)

    spread[...] = jnp.zeros_like(spread)
    names = lax.broadcasted_iota(jnp.int32, (slots, TILE), 1)
    for t in range(links):
        spread[t * 16 : t * 16 + slots, :] = (ids_v[:, t : t + 1] == names).astype(F32)

    def scale_row(name, keep):
        row = scaling[pl.ds(jnp.minimum(name, scen_count - 1), 1), :]
        return row * keep.astype(F32)

    total[...] = jnp.zeros_like(total)
    scaling_copy.wait()

    def add_slot(c):
        name = ids_s[c, me_t]
        row = scale_row(name, (name < scen_count).astype(jnp.int32))
        terms = []
        for at in range(0, width, TILE):
            block = rows[c, at : at + TILE, :]
            scaled = (block.T.astype(F32) * row[:, at : at + TILE]).astype(BF16)
            terms.append(jnp.dot(scaled, block, preferred_element_type=F32))
        summed = terms[0]
        for term in terms[1:]:
            summed = summed + term
        total[...] += summed

    def arrived(c):
        row_copy(c).wait()

        @pl.when(c + AHEAD < slots)
        def _():
            row_copy(c + AHEAD).start()

    early = slots - AHEAD

    @pl.loop(0, early)
    def _(c):
        arrived(c)
        add_slot(c)

    @pl.loop(early, slots)
    def _(c):
        arrived(c)

    part_width = width // 2
    up_row = scale_row(ids_s[up_slot, me_t], up_found)
    for at in range(0, part_width, TILE):
        down_send[at : at + TILE, :] = rows[down_slot, at : at + TILE, :]
    for at in range(0, part_width, TILE):
        beyond = part_width + at
        block = rows[up_slot, beyond : beyond + TILE, :]
        scaled = (block.T.astype(F32) * up_row[:, beyond : beyond + TILE]).astype(BF16)
        for inner in range(0, TILE, part_width // PIECES):
            up_send[(at + inner) // (part_width // PIECES)] = scaled[
                :, inner : inner + part_width // PIECES
            ]

    pl.semaphore_wait(barrier, 3 * (scens - 1) + links - 1)

    piece = part_width // PIECES
    seam = scens == 16 and links == 16

    def at_seam(side):
        return (me_t == links // 2 - side) if seam else (me_t < 0)

    def row_pieces(side, at, count):
        if side == 0:
            span = pl.ds(at * piece, count * piece)
            source, target = down_send.at[span], down_got.at[span]
            sems, peer = down_sems, link_source(1)
        else:
            span = pl.ds(at, count)
            source, target = up_send.at[span], up_got.at[span]
            sems, peer = up_sems, link_peer(1)
        return pltpu.make_async_remote_copy(
            src_ref=source,
            dst_ref=target,
            send_sem=sems.at[0],
            recv_sem=sems.at[1],
            device_id={"link": peer},
            device_id_type=MESH,
        )

    down_copy = row_pieces(0, 0, PIECES)
    up_copy = row_pieces(1, 0, PIECES)

    def seam_rows(first, last):
        for side in range(2):

            @pl.when(at_seam(side))
            def _():
                for at in range(first, last):
                    row_pieces(side, at, 1).start()

    @pl.when((me_t > 0) & jnp.logical_not(at_seam(0)))
    def _():
        down_copy.start()

    @pl.when((me_t + 1 < links) & jnp.logical_not(at_seam(1)))
    def _():
        up_copy.start()

    if seam:
        seam_rows(0, FIRST)

    for at in range(0, part_width, TILE):
        block = rows[up_slot, at : at + TILE, :]
        up_keep[:, at : at + TILE] = (
            block.T.astype(F32) * up_row[:, at : at + TILE]
        ).astype(BF16)

    @pl.loop(early, slots)
    def _(c):
        add_slot(c)

    low, high = total[:HALF, :HALF], total[HALF:, HALF:]
    part[:HALF, :] = 0.5 * (low + low.T)
    part[HALF : 2 * HALF, :] = 0.5 * (total[HALF:, :HALF] + total[:HALF, HALF:].T)
    part[2 * HALF :, :] = 0.5 * (high + high.T)

    def part_copy(k):
        peer = scen_peer(k)
        return pltpu.make_async_remote_copy(
            src_ref=part.at[pl.ds(pl.multiple_of(peer * chunk, 8), chunk)],
            dst_ref=gathered.at[me_s],
            send_sem=part_send,
            recv_sem=part_recv,
            device_id={"scen": peer},
            device_id_type=MESH,
        )

    def whole(ref, send_sem, recv_sem):
        return pltpu.make_async_remote_copy(
            src_ref=ref,
            dst_ref=ref,
            send_sem=send_sem,
            recv_sem=recv_sem,
            device_id={"scen": scen_peer(1)},
            device_id_type=MESH,
        )

    others = scens - 1
    part_all = whole(part.at[pl.ds(0, others * chunk)], part_send, part_recv)
    full_all = whole(full.at[pl.ds(0, others * chunk)], full_send, full_recv)
    upart_all = whole(upper_part.at[pl.ds(0, others * uchunk)], upart_send, upart_recv)
    bpart_all = whole(below_part, bpart_send, bpart_recv)
    ufull_all = whole(upper_full.at[pl.ds(0, others * uchunk)], ufull_send, ufull_recv)
    slot_all = whole(slot_send.at[pl.ds(0, links - 1)], slot_send_sems, slot_recv_sems)

    def full_copy(k):
        mine = pl.ds(pl.multiple_of(me_s * chunk, 8), chunk)
        return pltpu.make_async_remote_copy(
            src_ref=full.at[mine],
            dst_ref=full.at[mine],
            send_sem=full_send,
            recv_sem=full_recv,
            device_id={"scen": scen_peer(k)},
            device_id_type=MESH,
        )

    def upart_copy(k):
        peer = scen_peer(k)
        return pltpu.make_async_remote_copy(
            src_ref=upper_part.at[pl.ds(pl.multiple_of(peer * uchunk, 16), uchunk)],
            dst_ref=upper_gathered.at[me_s],
            send_sem=upart_send,
            recv_sem=upart_recv,
            device_id={"scen": peer},
            device_id_type=MESH,
        )

    def bpart_copy(k):
        peer = scen_peer(k)
        return pltpu.make_async_remote_copy(
            src_ref=below_part.at[pl.ds(pl.multiple_of(peer * uchunk, 16), uchunk)],
            dst_ref=upper_gathered.at[scens + me_s],
            send_sem=bpart_send,
            recv_sem=bpart_recv,
            device_id={"scen": peer, "link": link_source(1)},
            device_id_type=MESH,
        )

    def ufull_copy(k):
        mine = pl.ds(pl.multiple_of(me_s * uchunk, 16), uchunk)
        return pltpu.make_async_remote_copy(
            src_ref=upper_full.at[mine],
            dst_ref=upper_full.at[mine],
            send_sem=ufull_send,
            recv_sem=ufull_recv,
            device_id={"scen": scen_peer(k)},
            device_id_type=MESH,
        )

    @pl.loop(1, scens)
    def _(k):
        part_copy(k).start()

    if seam:
        seam_rows(FIRST, SECOND)

    gathered[me_s] = part[pl.ds(pl.multiple_of(me_s * chunk, 8), chunk), :]

    part_all.wait_recv()

    full[pl.ds(pl.multiple_of(me_s * chunk, 8), chunk), :] = tree_sum(
        [gathered[i] for i in range(scens)]
    )

    @pl.loop(1, scens)
    def _(k):
        full_copy(k).start()

    if seam:
        seam_rows(SECOND, PIECES)

    full_all.wait_recv()

    corner = full[HALF : 2 * HALF, :]
    matrix[:HALF, :HALF] = full[:HALF, :]
    matrix[HALF:, :HALF] = corner
    matrix[:HALF, HALF:] = corner.T
    matrix[HALF:, HALF:] = full[2 * HALF :, :]
    on_diag = lax.broadcasted_iota(jnp.int32, (TILE, TILE), 0) == lax.broadcasted_iota(
        jnp.int32, (TILE, TILE), 1
    )
    matrix[...] += jnp.where(on_diag, regulariser[...], 0.0)

    def store_wide(ref, value):
        ref[:TILE, :] = value[:, :HALF].astype(BF16)
        ref[TILE:, :] = value[:, HALF:].astype(BF16)

    def below_terms():
        @pl.when(me_t > 0)
        def _():
            up_copy.wait_recv()
            scaled = jnp.concatenate([up_got[i] for i in range(PIECES)], axis=1)
            store_wide(
                below_part,
                jnp.dot(scaled, rows[down_slot, part_width:, :], preferred_element_type=F32),
            )

            @pl.loop(0, scens)
            def _(k):
                bpart_copy(k).start()

    def upper_terms():
        @pl.when(me_t + 1 < links)
        def _():
            down_copy.wait_recv()
            store_wide(
                upper_part,
                jnp.dot(up_keep[...], down_got[...], preferred_element_type=F32),
            )

            @pl.loop(1, scens)
            def _(k):
                upart_copy(k).start()

            upper_gathered[me_s] = upper_part[
                pl.ds(pl.multiple_of(me_s * uchunk, 16), uchunk), :
            ]

    def upper_sum():
        @pl.when(me_t + 1 < links)
        def _():
            upart_all.wait_recv()
            bpart_all.wait_recv()

            upper_full[pl.ds(pl.multiple_of(me_s * uchunk, 16), uchunk), :] = tree_sum(
                [upper_gathered[i].astype(F32) for i in range(2 * scens)]
            ).astype(BF16)

            @pl.loop(1, scens)
            def _(k):
                ufull_copy(k).start()

    for at in range(0, TILE, PANEL):
        sweep_rows(matrix, at)
        turn = at // PANEL
        if turn == 0:
            pl.when(jnp.logical_not(at_seam(0)))(below_terms)
            pl.when(jnp.logical_not(at_seam(1)))(upper_terms)
        if seam and turn == BELOW_TURN:
            pl.when(at_seam(0))(below_terms)
        if seam and turn == UPPER_TURN:
            pl.when(at_seam(1))(upper_terms)
        if at == 4 * PANEL:
            pl.when(jnp.logical_not(at_seam(1)))(upper_sum)

    if seam:
        pl.when(at_seam(1))(upper_sum)

    def solve(vector):
        wide = jnp.broadcast_to(vector, (8, TILE))
        found = -jnp.dot(wide, matrix[...], precision=HIGHEST, preferred_element_type=F32)
        return found[:1, :]

    def split(vector):
        first = vector.astype(BF16)
        left = vector - first.astype(F32)
        second = left.astype(BF16)
        third = (left - second.astype(F32)).astype(BF16)
        parts = [jnp.broadcast_to(v.astype(F32), (8, TILE)) for v in (first, second, third)]
        sub = lax.broadcasted_iota(jnp.int32, (8, TILE), 0)
        mixed = jnp.where(sub == 0, parts[0], jnp.where(sub == 1, parts[1], parts[2]))
        return jnp.where(sub < 3, mixed, 0.0).astype(BF16)

    def to_next(vector):
        parts = split(vector)
        low = jnp.dot(parts, upper_full[:TILE, :], preferred_element_type=F32)
        high = jnp.dot(parts, upper_full[TILE:, :], preferred_element_type=F32)
        return jnp.sum(jnp.concatenate([low, high], axis=1), axis=0, keepdims=True)

    def from_next(vector):
        parts = split(vector)
        turned = (((1,), (1,)), ((), ()))
        low = lax.dot_general(
            parts[:, :HALF], upper_full[:TILE, :], turned, preferred_element_type=F32
        )
        high = lax.dot_general(
            parts[:, HALF:], upper_full[TILE:, :], turned, preferred_element_type=F32
        )
        return jnp.sum(low + high, axis=0, keepdims=True)

    def put(ref, vector):
        ref[0:1, :] = vector[:, :HALF]
        ref[1:2, :] = vector[:, HALF:]

    def fetch(ref):
        return jnp.concatenate([ref[0:1, :], ref[1:2, :]], axis=1)

    lane_count = 4
    lane = lax.rem(me_s, lane_count)
    first_lane = me_s - lane

    def vec_copy(step, side, extra):
        cross = at_seam(side)
        if extra:
            target = first_lane + jnp.where(lane == 0, 2, 1)
        else:
            target = jnp.where(cross, first_lane + lane_count - 1 - lane, me_s)
        slot = 2 * step + side
        return pltpu.make_async_remote_copy(
            src_ref=vec_send.at[slot],
            dst_ref=vec_recv.at[slot],
            send_sem=vsend_sems.at[2 * slot + extra],
            recv_sem=vrecv_sems.at[slot],
            device_id={
                "scen": target,
                "link": link_source(1) if side == 0 else link_peer(1),
            },
            device_id_type=MESH,
        )

    def vec_act(step, side, act):
        cross = at_seam(side)
        edge = (lane == 0) | (lane == lane_count - 1)

        @pl.when(jnp.logical_not(cross) | edge)
        def _():
            act(vec_copy(step, side, 0))

        if seam:

            @pl.when(cross & edge)
            def _():
                act(vec_copy(step, side, 1))

    colour = lax.rem(me_t, 2)
    vec_send[...] = jnp.zeros_like(vec_send)
    current[...] = jnp.zeros_like(current)

    @pl.when(colour == 0)
    def _():
        current[...] = solve(right_side[...])

    @pl.when(me_t + 1 < links)
    def _():
        ufull_all.wait_recv()

    for step in range(2 * SWEEPS - 1):

        @pl.when(colour == step % 2)
        def _():
            @pl.when(me_t > 0)
            def _():
                put(vec_send.at[2 * step], current[...])
                vec_act(step, 0, lambda copy: copy.start())

            @pl.when(me_t + 1 < links)
            def _():
                put(vec_send.at[2 * step + 1], to_next(current[...]))
                vec_act(step, 1, lambda copy: copy.start())

        @pl.when(colour != step % 2)
        def _():
            current[...] = right_side[...]

            @pl.when(me_t + 1 < links)
            def _():
                vec_copy(step, 0, 0).wait_recv()
                current[...] -= from_next(fetch(vec_recv.at[2 * step]))

            @pl.when(me_t > 0)
            def _():
                vec_copy(step, 1, 0).wait_recv()
                current[...] -= fetch(vec_recv.at[2 * step + 1])

            current[...] = solve(current[...])

    direction_out[...] = current[...]

    rounded = current[...].astype(BF16)
    half = jnp.broadcast_to(rounded, (16, TILE))
    direct = rounded.astype(F32)

    def slot_order(k):
        if not seam:
            return lax.rem(me_t + k + 1, links)
        block = links // 2
        near = jnp.where(k < 12, k - 4, jnp.where(k < 15, k - 11, 0))
        turn = jnp.where(k < block, k, near)
        side = me_t // block
        side = jnp.where(k < block, 1 - side, side)
        return side * block + lax.rem(me_t + turn, block)

    def slot_copy(k):
        peer = slot_order(k)
        return pltpu.make_async_remote_copy(
            src_ref=slot_send.at[peer],
            dst_ref=slot_recv.at[me_t],
            send_sem=slot_send_sems,
            recv_sem=slot_recv_sems,
            device_id={"link": peer},
            device_id_type=MESH,
        )

    @pl.loop(0, links)
    def _(k):
        peer = slot_order(k)
        at = pl.ds(pl.multiple_of(peer * pieces, HALF), pieces)
        values = []
        for c in range(slots):
            block = rows[c, at, :]
            if c % 2:
                value = block.astype(F32) * direct
                value = value[:, :HALF] + value[:, HALF:]
                values.append(jnp.sum(value.T, axis=0, keepdims=True))
            else:
                value = lax.dot_general(
                    half, block, (((1,), (1,)), ((), ())), preferred_element_type=F32
                )
                values.append(value[:1, :])
        values.append(jnp.zeros((16 - slots, pieces), F32))
        slot_send[peer] = jnp.concatenate(values, axis=0)

        @pl.when(k + 1 < links)
        def _():
            slot_copy(k).start()

    slot_recv[me_t] = slot_send[me_t]

    slot_all.wait_recv()

    values = slot_recv[...].reshape(links * 16, pieces)
    summed = dot_tt(spread[...], values)
    columns = scaling[:, pl.ds(pl.multiple_of(me_t * pieces, HALF), pieces)]
    step_out[...] = columns * summed[:scen_count, :]

    part_all.wait_send()
    full_all.wait_send()

    @pl.when(me_t + 1 < links)
    def _():
        up_copy.wait_send()

        upart_all.wait_send()
        ufull_all.wait_send()

    @pl.when(me_t > 0)
    def _():
        down_copy.wait_send()

        bpart_all.wait_send()

    for step in range(2 * SWEEPS - 1):

        @pl.when(colour == step % 2)
        def _():
            @pl.when(me_t > 0)
            def _():
                vec_act(step, 0, lambda copy: copy.wait_send())

            @pl.when(me_t + 1 < links)
            def _():
                vec_act(step, 1, lambda copy: copy.wait_send())

    slot_all.wait_send()


def hand_over(direction, step, direction_out, step_out):
    direction_out[...] = direction[...]
    step_out[...] = step[...]


def shards(link_rows, slot_scenario, diag_scaling, regulariser, right_side):
    scens, links = lax.axis_size("scen"), lax.axis_size("link")
    slots, width, _ = link_rows.shape
    scen_count = diag_scaling.shape[0]
    pieces = width // links
    steps = 2 * SWEEPS - 1
    vmem = pl.BlockSpec(memory_space=pltpu.VMEM)
    dma = pltpu.SemaphoreType.DMA
    direction, step = pl.pallas_call(
        functools.partial(kernel, scens, links),
        out_shape=(
            pltpu.VMEM((1, TILE), F32),
            pltpu.VMEM((scen_count, pieces), F32),
        ),
        in_specs=[
            pl.BlockSpec(memory_space=pltpu.SMEM),
            vmem,
            pl.BlockSpec(memory_space=pl.ANY),
            pl.BlockSpec(memory_space=pl.ANY),
            vmem,
            vmem,
        ],
        out_specs=(vmem, vmem),
        scratch_shapes=[
            pltpu.VMEM((slots, width, TILE), BF16),
            pltpu.VMEM((scen_count, width), F32),
            pltpu.VMEM((TILE, TILE), F32),
            pltpu.VMEM((3 * HALF, HALF), F32),
            pltpu.VMEM((scens, 3 * HALF // scens, HALF), F32),
            pltpu.VMEM((3 * HALF, HALF), F32),
            pltpu.VMEM((TILE, TILE), F32),
            pltpu.VMEM((TILE, width // 2), BF16),
            pltpu.VMEM((PIECES, TILE, width // 2 // PIECES), BF16),
            pltpu.VMEM((PIECES, TILE, width // 2 // PIECES), BF16),
            pltpu.VMEM((width // 2, TILE), BF16),
            pltpu.VMEM((width // 2, TILE), BF16),
            pltpu.VMEM((2 * TILE, HALF), BF16),
            pltpu.VMEM((2 * TILE, HALF), BF16),
            pltpu.VMEM((2 * scens, 2 * TILE // scens, HALF), BF16),
            pltpu.VMEM((2 * TILE, HALF), BF16),
            pltpu.VMEM((1, TILE), F32),
            pltpu.VMEM((2 * steps, 8, HALF), F32),
            pltpu.VMEM((2 * steps, 8, HALF), F32),
            pltpu.VMEM((links * 16, TILE), F32),
            pltpu.VMEM((links, 16, pieces), F32),
            pltpu.VMEM((links, 16, pieces), F32),
            dma((slots,)),
            dma,
            dma,
            dma,
            dma,
            dma,
            dma((2,)),
            dma((2,)),
            dma,
            dma,
            dma,
            dma,
            dma,
            dma,
            dma((4 * steps,)),
            dma((2 * steps,)),
            dma,
            dma,
        ],
        compiler_params=pltpu.CompilerParams(
            collective_id=0, has_side_effects=True, vmem_limit_bytes=56 * 2**20
        ),
        name="coloured_sweeps",
    )(
        slot_scenario,
        slot_scenario,
        link_rows,
        diag_scaling,
        regulariser.reshape(1, TILE),
        right_side.reshape(1, TILE),
    )
    direction, step = pl.pallas_call(
        hand_over,
        out_shape=(
            jax.ShapeDtypeStruct((1, TILE), F32),
            jax.ShapeDtypeStruct((scen_count, pieces), F32),
        ),
        in_specs=[vmem, vmem],
        out_specs=(vmem, vmem),
        compiler_params=pltpu.CompilerParams(vmem_limit_bytes=2**20),
        name="hand_over",
    )(direction, step)
    return direction.reshape(TILE), step


def solution(mesh):
    in_specs = (P("scen", None, "link"), P("scen", None), P("scen", None), P("link"), P("link"))
    out_specs = (P("link"), P("scen", "link"))
    return jax.shard_map(shards, mesh=mesh, in_specs=in_specs, out_specs=out_specs, check_vma=False)
```
